32 devices in a mesh: dp: 8 (over z, y), head: 4 (over x, core).
Axes of the slice: x: 2, y: 2, z: 4, core: 2. Of those that a mesh axis runs over, the one named last changes fastest.
Arguments:
- layer_input: bfloat16 [16, 2048, 768], P('dp', 'head'), may hold values from -6 to 6
- doc_lengths: int32 [16, 6], P('dp'), may hold values from 1 to 1024, 2048 in all within a row
- ln1_gain: bfloat16 [2, 768], P(None, 'dp'), may hold values from 0.5 to 1.5
- ln1_bias: bfloat16 [2, 768], P(None, 'dp'), may hold values from -1.5 to 1.5
- qkv_weight: bfloat16 [2, 768, 2304], P(None, 'dp', 'head'), may hold values from -0.0625 to 0.0625
- out_weight: bfloat16 [2, 768, 768], P(None, 'head', 'dp'), may hold values from -2 to 2
- ln2_gain: bfloat16 [2, 768], P(None, 'dp'), may hold values from 0.5 to 1.5
- ln2_bias: bfloat16 [2, 768], P(None, 'dp'), may hold values from -1.5 to 1.5
- in_weight: bfloat16 [2, 768, 3072], P(None, 'dp', 'head'), may hold values from -0.21875 to 0.21875
- down_weight: bfloat16 [2, 3072, 768], P(None, 'head', 'dp'), may hold values from -0.109375 to 0.109375
- cotangent: bfloat16 [16, 2048, 768], P('dp', 'head'), may hold values from -6 to 6
Outputs:
- layer_output: bfloat16 [16, 2048, 768], P('dp', 'head')
- input_grad: float32 [16, 2048, 768], P('dp', 'head')
- ln1_gain_grad: float32 [2, 768], P(None, ('dp', 'head'))
- ln1_bias_grad: float32 [2, 768], P(None, ('dp', 'head'))
- qkv_grad: float32 [2, 768, 2304], P(None, 'dp', 'head')
- out_grad: float32 [2, 768, 768], P(None, 'head', 'dp')
- ln2_gain_grad: float32 [2, 768], P(None, ('dp', 'head'))
- ln2_bias_grad: float32 [2, 768], P(None, ('dp', 'head'))
- in_grad: float32 [2, 768, 3072], P(None, 'dp', 'head')
- down_grad: float32 [2, 3072, 768], P(None, 'head', 'dp')
The draws below stay inside these ranges and needn't reach their ends.
Inputs may be any that keep to these rules, and one draw needn't show every extreme that they name: `doc_lengths`: each row's 6 lengths sum to 2048, and the largest of them is exactly 1024.
All inputs are finite; a program needn't handle non-finite values.
Results may differ from the reference program's by a relative error of at most 0.014.
Values may be sent and summed in bfloat16 or wider, within the bound.
No kernel may reach another device: no remote copies, remote signals or barrier semaphores. Data moves between devices by JAX's collectives and lax.ppermute only.
A program may use at most 448 MiB of HBM per device.

```python
import math
import jax
import jax.numpy as jnp
import numpy as np
from jax import lax

D = 768
HEADS = 12
HD = 64
FF = 3072
LAYERS = 2
ROW = 2048
BLOCK = 512
NDOC = 6
MOST = 1024
ROWS = 16
N_HEAD = 4


def spiked(values, own_key, source, target, blocks, factor):
    def block_of(dim):
        return (jnp.arange(values.shape[dim]) // (values.shape[dim] // blocks)).reshape((-1,) + (1,) * (values.ndim - 1 - dim))

    first = jax.random.permutation(own_key, blocks)[block_of(target)]
    other_side = (block_of(target) + blocks // 2) % blocks
    return jnp.where((block_of(source) == first) | (block_of(source) == other_side), factor * values, values)


def block_scale(own_key, dims, shards, low, top_value):
    level, own = 1.0, jax.random.fold_in(own_key, 6)
    for axis_at, blocks in shards:
        draws = jnp.exp(jax.random.uniform(jax.random.fold_in(own, axis_at), (blocks,), jnp.float32, low / len(shards), top_value / len(shards)))
        level = level * jnp.repeat(draws, dims[axis_at] // blocks).reshape([-1 if axis == axis_at else 1 for axis in range(len(dims))])
    return level


def split_up(count, total, reach, lean):
    portions = [(1 << 20) // math.isqrt(standing ** lean) + 1 for standing in range(2, count + 1)]
    rest, counts = total - reach - (count - 1), [1] * (count - 1)
    while rest > 0:
        candidates = [i for i in range(count - 1) if counts[i] < reach]
        mass, remaining = sum([portions[i] for i in candidates]), rest
        for i in candidates:
            addition = min(reach - counts[i], max(1, remaining * portions[i] // mass), rest)
            counts[i] = counts[i] + addition
            rest = rest - addition
    return np.array([reach] + counts)


def uneven_parts(own_key, count, total, reach, skew):
    if count == 2:
        one = jax.random.randint(own_key, (), max(1, total - reach), min(reach, total - 1) + 1)
        return jnp.stack([one, total - one])
    tallies = jnp.asarray(split_up(count, total, reach, skew), jnp.int32)
    twos = (count - 1) // 2
    source_of, receiver = tallies[1:1 + 2 * twos:2], tallies[2:2 + 2 * twos:2]
    slack = jnp.minimum(source_of - 1, reach - receiver)
    moved = jax.random.randint(jax.random.fold_in(own_key, 1), (twos,), 0, 1 << 20) % (slack + 1)
    tallies = tallies.at[1:1 + 2 * twos:2].set(source_of - moved).at[2:2 + 2 * twos:2].set(receiver + moved)
    return tallies[jax.random.permutation(jax.random.fold_in(own_key, 2), count)]


def normal_values(rng, dims, deviation, most, cuts=(), held_as=jnp.bfloat16):
    values = jax.random.normal(rng, dims, jnp.float32) * deviation
    if len(cuts) > 0:
        values = block_scale(rng, dims, cuts, -0.22, 0.18) * values
    return jnp.clip(values, min=-most, max=most).astype(held_as)


def noise_with(stream_key, dims, deviation, bound, cuts, heavy, kind=jnp.bfloat16):
    entries = deviation * jax.random.normal(stream_key, dims, jnp.float32)
    if cuts:
        entries = entries * block_scale(stream_key, dims, cuts, -0.22, 0.18)
    return jnp.clip(spiked(entries, jax.random.fold_in(stream_key, 3), *heavy), -bound, bound).astype(kind)


def setup_inputs(seed: int = 0) -> dict:
    seeds = jax.random.split(jax.random.key(seed), 12)
    return {
        "layer_input": noise_with(seeds[0], (ROWS, ROW, D), 1.0, 6.0, ((0, 8), (1, 4)), (0, 2, 8, 2.0)),
        "doc_lengths": jax.vmap(lambda own: uneven_parts(own, NDOC, ROW, MOST, 2))(jax.random.split(seeds[1], ROWS)).reshape((ROWS, NDOC)).astype(jnp.int32),
        "ln1_gain": jnp.clip(0.5 + 1.0 * jax.random.uniform(seeds[2], (LAYERS, D), jnp.float32) ** block_scale(seeds[2], (LAYERS, D), ((1, 8),), -0.2, 0.2), 0.5, 1.5).astype(jnp.bfloat16),
        "ln1_bias": normal_values(seeds[3], (LAYERS, D), 0.3, 1.5, ((1, 8),)),
        "qkv_weight": normal_values(seeds[4], (LAYERS, D, 3 * D), (12 * D) ** -0.5, 0.0625, ((1, 8), (2, 4))),
        "out_weight": normal_values(seeds[5], (LAYERS, D, D), (D // 96) ** -0.5, 2.0, ((1, 4), (2, 8))),
        "ln2_gain": jnp.clip(0.5 + 1.0 * jax.random.uniform(seeds[6], (LAYERS, D), jnp.float32) ** block_scale(seeds[6], (LAYERS, D), ((1, 8),), -0.2, 0.2), 0.5, 1.5).astype(jnp.bfloat16),
        "ln2_bias": normal_values(seeds[7], (LAYERS, D), 0.3, 1.5, ((1, 8),)),
        "in_weight": normal_values(seeds[8], (LAYERS, D, FF), D ** -0.5, 0.21875, ((1, 8), (2, 4))),
        "down_weight": normal_values(seeds[9], (LAYERS, FF, D), FF ** -0.5, 0.109375, ((1, 4), (2, 8))),
        "cotangent": noise_with(seeds[10], (ROWS, ROW, D), 1.0, 6.0, ((0, 8), (1, 4)), (0, 2, 8, 2.0)),
    }


@jax.custom_vjp
def low(v):
    return lax.optimization_barrier(v.astype(jnp.bfloat16)).astype(jnp.float32)

@jax.custom_vjp
def low_back(v):
    return v

def low_keep(v):
    return (low(v), None)

def low_pass(kept, grad):
    return (grad,)

def back_keep(v):
    return (v, None)

def back_low(kept, grad):
    return (low(grad),)
low.defvjp(low_keep, low_pass)
low_back.defvjp(back_keep, back_low)
NORM_EPS = 1e-05
HIGHEST_PRECISION = lax.Precision.HIGHEST

def doc_place(lengths_row):
    doc_ends = jnp.cumsum(lengths_row).astype(jnp.int32)
    doc_starts = (doc_ends - lengths_row).astype(jnp.int32)
    position = jnp.arange(ROW, dtype=jnp.int32)
    inside = ((position[:, None] >= doc_starts[None, :]) & (position[:, None] < doc_ends[None, :])).astype(jnp.int32)
    labels = jnp.arange(lengths_row.shape[0], dtype=jnp.int32)
    doc_index = lax.optimization_barrier(jnp.sum(inside * labels[None, :], axis=1)).astype(jnp.int32)
    doc_start = lax.optimization_barrier(jnp.sum(inside * doc_starts[None, :], axis=1))
    doc_size = lax.optimization_barrier(jnp.sum(inside * lengths_row[None, :], axis=1))
    angles = math.pi / 2 * (position - doc_start).astype(jnp.float32) / doc_size.astype(jnp.float32)
    return (doc_index, angles)

def layer_norm(stream, gain_vec, bias_vec):
    average = lax.optimization_barrier(jnp.mean(stream, axis=-1, keepdims=True))
    centered = stream - average
    variance = lax.optimization_barrier(jnp.mean(centered * centered, axis=-1, keepdims=True))
    return centered * lax.rsqrt(variance + NORM_EPS) * gain_vec + bias_vec

def features(values, angles):
    positive = jax.nn.relu(values)
    return jnp.concatenate([positive * jnp.cos(angles)[:, None, None], positive * jnp.sin(angles)[:, None, None]], axis=-1)

def attend(query_rows, key_rows, value_rows, doc_index, angles):
    row_count, heads_here, head_width = value_rows.shape
    blocks = row_count // BLOCK
    query_feat = features(query_rows, angles).reshape(blocks, BLOCK, heads_here, 2 * head_width)
    key_feat = features(key_rows, angles).reshape(blocks, BLOCK, heads_here, 2 * head_width)
    value_blocks = value_rows.reshape(blocks, BLOCK, heads_here, head_width)
    doc_blocks = doc_index.reshape(blocks, BLOCK)
    causal = jnp.arange(BLOCK)[:, None] >= jnp.arange(BLOCK)[None, :]

    def block_step(carried_in, pieces):
        kv_state, key_total, last_doc = carried_in
        query_block, key_block, value_block, doc_block = pieces
        same_doc = ((doc_block[:, None] == doc_block[None, :]) & causal).astype(jnp.float32)
        weights = jnp.einsum('ihf,jhf->hij', query_block, key_block, precision=HIGHEST_PRECISION) * same_doc[None]
        numerator = jnp.einsum('hij,jhe->ihe', weights, value_block, precision=HIGHEST_PRECISION)
        denominator = lax.optimization_barrier(jnp.sum(weights, axis=2)).T
        from_before = (doc_block == last_doc).astype(jnp.float32)[:, None]
        numerator = numerator + from_before[:, :, None] * jnp.einsum('ihf,hfe->ihe', query_block, kv_state, precision=HIGHEST_PRECISION)
        denominator = denominator + from_before * jnp.einsum('ihf,hf->ih', query_block, key_total, precision=HIGHEST_PRECISION)
        attended = numerator / (denominator + 1.0)[:, :, None]
        tail_doc = doc_block[BLOCK - 1]
        keep_flag = (last_doc == tail_doc).astype(jnp.float32)
        member = (doc_block == tail_doc).astype(jnp.float32)[:, None, None]
        masked = key_block * member
        kv_state = keep_flag * kv_state + jnp.einsum('jhf,jhe->hfe', masked, value_block, precision=HIGHEST_PRECISION)
        key_total = keep_flag * key_total + lax.optimization_barrier(jnp.sum(masked, axis=0))
        return ((kv_state, key_total, tail_doc), attended)
    initial = (jnp.zeros((heads_here, 2 * head_width, head_width), jnp.float32), jnp.zeros((heads_here, 2 * head_width), jnp.float32), jnp.array(-1, dtype=jnp.int32))
    _, attended = lax.scan(jax.checkpoint(block_step), initial, (query_feat, key_feat, value_blocks, doc_blocks))
    return attended.reshape(row_count, heads_here, head_width)

def layer(stream, weights, doc_index, angles):
    gain_one, bias_one, qkv_w, out_w, gain_two, bias_two, in_w, down_w = weights
    row_count = stream.shape[0]
    heads_here = HEADS // N_HEAD
    qkv_cols = 3 * D // N_HEAD
    out_rows = D // N_HEAD
    normed = low(layer_norm(stream, gain_one, bias_one))
    pieces = []
    for group_index in range(N_HEAD):
        mixed = jnp.einsum('rtd,dc->rtc', normed, qkv_w[:, group_index * qkv_cols:(group_index + 1) * qkv_cols], precision=HIGHEST_PRECISION)
        mixed = low_back(low(mixed)).reshape(row_count, ROW, 3, heads_here, HD)
        attended = jax.vmap(attend)(mixed[:, :, 0], mixed[:, :, 1], mixed[:, :, 2], doc_index, angles)
        pieces.append(attended.reshape(row_count, ROW, out_rows))
    attended_all = low(jnp.concatenate(pieces, axis=-1))
    branch = jnp.einsum('rtc,cd->rtd', attended_all, out_w, precision=HIGHEST_PRECISION)
    stream = stream + low_back(branch)
    normed = low(layer_norm(stream, gain_two, bias_two))
    pre_act = low_back(jnp.einsum('rtd,dc->rtc', normed, in_w, precision=HIGHEST_PRECISION))
    act_low = low(jax.nn.gelu(pre_act))
    branch = jnp.einsum('rtc,cd->rtd', act_low, down_w, precision=HIGHEST_PRECISION)
    return stream + low_back(branch)

def forward(stream, weights, doc_index, angles):
    for layer_index in range(LAYERS):
        stream = layer(stream, tuple((member[layer_index] for member in weights)), doc_index, angles)
    return stream

def reference(layer_input, doc_lengths, ln1_gain, ln1_bias, qkv_weight, out_weight, ln2_gain, ln2_bias, in_weight, down_weight, cotangent):
    weights = tuple((member.astype(jnp.float32) for member in (ln1_gain, ln1_bias, qkv_weight, out_weight, ln2_gain, ln2_bias, in_weight, down_weight)))
    pair_count = layer_input.shape[0] // 2
    inputs = layer_input.astype(jnp.float32).reshape(pair_count, 2, ROW, D)
    cotangents = cotangent.astype(jnp.float32).reshape(pair_count, 2, ROW, D)
    lengths = doc_lengths.reshape(pair_count, 2, doc_lengths.shape[1])

    def row_group(summed, pieces):
        input_pair, cot_pair, length_pair = pieces
        doc_index, angles = jax.vmap(doc_place)(length_pair)

        def run_layers(stream, params):
            return forward(stream, params, doc_index, angles)
        result, backward = jax.vjp(run_layers, input_pair, weights)
        input_part, weight_parts = backward(cot_pair)
        summed = tuple((left + right for left, right in zip(summed, weight_parts)))
        return (summed, (result.astype(jnp.bfloat16), input_part))
    zeroes = tuple((jnp.zeros_like(member) for member in weights))
    summed, (outputs, input_parts) = lax.scan(row_group, zeroes, (inputs, cotangents, lengths))
    return (outputs.reshape(layer_input.shape), input_parts.reshape(layer_input.shape), summed[0], summed[1], summed[2], summed[3], summed[4], summed[5], summed[6], summed[7])
```

```python
import math

import jax
import jax.numpy as jnp
from jax import lax
from jax.sharding import PartitionSpec as P

HD = 64
ROW = 2048
NORM_EPS = 1e-05
BF = jnp.bfloat16
F32 = jnp.float32


def xor_groups(n):
    groups, span = [[1]], 2
    while span < n:
        radix = min(4, n // span)
        groups.append([span * k for k in range(1, radix)])
        span *= radix
    return groups[::-1]


def swap(x, axis, mask):
    n = lax.axis_size(axis)
    return lax.ppermute(x, axis, [(i, i ^ mask) for i in range(n)])


def forward_shift(x, by):
    n = lax.axis_size("head")
    return lax.ppermute(x, "head", [(i, i + by) for i in range(n - by)])


def backward_shift(x, by):
    n = lax.axis_size("head")
    return lax.ppermute(x, "head", [(i + by, i) for i in range(n - by)])


def block_order(groups):
    order = [0]
    for masks in groups:
        order = order + [r ^ m for m in masks for r in order]
    return order


def spread(x, axis, masks, dim):
    return jnp.concatenate([x] + [swap(x, axis, m) for m in masks], axis=dim)


def pair_columns(own, other):
    pieces = []
    for at in range(0, own.shape[1], HD):
        pieces += [own[:, at : at + HD], other[:, at : at + HD]]
    return jnp.concatenate(pieces, axis=1)


def plain_columns(own, other):
    return jnp.concatenate([own, other], axis=1)


def gather(shard, groups, join, last):
    x = shard
    for masks in groups[:-1]:
        x = spread(x, "dp", masks, 0)
    if last == "x":
        x = spread(x, "dp", groups[-1], 0)
        half = join(x, swap(x, "head", 2))
    else:
        half = join(x, swap(x, "head", 2))
        half = spread(half, "dp", groups[-1], 0)
    return half, swap(half, "head", 1)


def split_pairs(x):
    own = [x[:, at : at + HD] for at in range(0, x.shape[1], 2 * HD)]
    other = [x[:, at + HD : at + 2 * HD] for at in range(0, x.shape[1], 2 * HD)]
    return jnp.concatenate(own, axis=1), jnp.concatenate(other, axis=1)


def split_plain(x):
    c = x.shape[1] // 2
    return x[:, :c], x[:, c:]


def add_rows(x, axis, masks):
    rows = x.shape[0] // (len(masks) + 1)
    total = x[:rows].astype(F32)
    for j, m in enumerate(masks):
        piece = x[(j + 1) * rows : (j + 2) * rows].astype(BF)
        total = total + swap(piece, axis, m).astype(F32)
    return total


def reduce_scatter(own, other, groups, split, first):
    total = own + swap(other.astype(BF), "head", 1).astype(F32)
    rest = groups[::-1]
    if first == "y":
        total = add_rows(total, "dp", rest[0])
        rest = rest[1:]
    keep, send = split(total)
    total = keep + swap(send.astype(BF), "head", 2).astype(F32)
    for masks in rest:
        total = add_rows(total, "dp", masks)
    return total


def norm(stream, gain, bias):
    mean = jnp.mean(stream, axis=-1, keepdims=True)
    centred = stream - mean
    rstd = lax.rsqrt(jnp.mean(centred * centred, axis=-1, keepdims=True) + NORM_EPS)
    return (centred * rstd * gain + bias).astype(BF), (mean, rstd)


def norm_back(stream, stats, gain, grad):
    mean, rstd = stats
    xhat = (stream - mean) * rstd
    gain_grad = jnp.sum(grad * xhat, axis=0)
    bias_grad = jnp.sum(grad, axis=0)
    g = grad * gain
    back = rstd * (
        g - jnp.mean(g, axis=-1, keepdims=True) - xhat * jnp.mean(g * xhat, axis=-1, keepdims=True)
    )
    return back, gain_grad, bias_grad


def gelu_and_slope(x):
    c = math.sqrt(2.0 / math.pi)
    t = jnp.tanh(c * (x + 0.044715 * (x * x * x)))
    half = 0.5 * (1.0 + t)
    slope = half + 0.5 * x * (1.0 - t * t) * (c * (1.0 + 3 * 0.044715 * (x * x)))
    return (x * half).astype(BF), slope.astype(BF)


def dot(a, b):
    return lax.dot_general(a, b, (((1,), (0,)), ((), ())), preferred_element_type=F32)


def dot_t(a, b):
    return lax.dot_general(a, b, (((1,), (1,)), ((), ())), preferred_element_type=F32)


def t_dot(a, b):
    return lax.dot_general(a, b, (((0,), (0,)), ((), ())), preferred_element_type=F32)


def places(lengths, position):
    n = lengths.shape[0]
    upto = jnp.arange(n)[:, None] <= jnp.arange(n)[None, :]
    ends = jnp.sum(jnp.where(upto, lengths[:, None], 0), axis=0)
    passed = (position[:, None] >= ends[None, :]).astype(jnp.int32)
    doc = jnp.sum(passed, axis=1)
    start = jnp.sum(passed * lengths[None, :], axis=1)
    here = (doc[:, None] == jnp.arange(n)[None, :]).astype(jnp.int32)
    size = jnp.sum(here * lengths[None, :], axis=1)
    return doc, start, size


STATE_ROWS = 144


def heads_of(x, b, rows):
    return x[b * rows : (b + 1) * rows].reshape(rows, -1, HD)


def qkv_of(mixed, b, rows):
    width = mixed.shape[1] // 3
    q, k, v = [heads_of(mixed[:, i * width : (i + 1) * width], b, rows) for i in range(3)]
    return jax.nn.relu(q).astype(F32), jax.nn.relu(k).astype(F32), v.astype(F32), q, k


def pack_state(kv, ks):
    heads = kv.shape[1]
    kv = kv.reshape(2, heads // 2, 2, HD, HD).transpose(1, 0, 3, 2, 4).reshape(heads // 2, 2 * HD, 2 * HD)
    ks = ks.reshape(2, heads // 2, 2 * HD).transpose(1, 0, 2)
    pad = jnp.zeros((heads // 2, STATE_ROWS - 2 * HD - 2, 2 * HD), F32)
    return jnp.concatenate([kv, ks, pad], axis=1).astype(BF)


def unpack_state(st):
    pairs = st.shape[0]
    st = st.astype(F32)
    kv = st[:, : 2 * HD].reshape(pairs, 2, HD, 2, HD).transpose(1, 0, 3, 2, 4).reshape(2, 2 * pairs, HD, HD)
    ks = st[:, 2 * HD : 2 * HD + 2].transpose(1, 0, 2).reshape(2, 2 * pairs, HD)
    return kv, ks


def local_state(mixed, info, rows):
    out = []
    for b in range(2):
        _, rk, v, _, _ = qkv_of(mixed, b, rows)
        w = jnp.stack([info["memcos"][b], info["memsin"][b]])
        kf = (w[:, :, None, None] * rk[None]).astype(BF)
        kv = jnp.einsum("stha,the->shae", kf, v.astype(BF), preferred_element_type=F32)
        ks = jnp.sum(kf.astype(F32), axis=1)
        out.append(pack_state(kv, ks))
    return jnp.stack(out)


def attend(mixed, state, info, rows):
    atts, dens = [], []
    for b in range(2):
        rq, rk, v, _, _ = qkv_of(mixed, b, rows)
        s = jnp.einsum("tha,uha->htu", rq.astype(BF), rk.astype(BF), preferred_element_type=F32)
        w = (s * info["mask"][b][None]).astype(BF)
        num = jnp.einsum("htu,uhe->the", w, v.astype(BF), preferred_element_type=F32)
        den = jnp.sum(w.astype(F32), axis=2).T
        kv, ks = unpack_state(state[b])
        f = jnp.stack([info["fbcos"][b], info["fbsin"][b]])
        qf = (f[:, :, None, None] * rq[None]).astype(BF)
        num = num + jnp.einsum("stha,shae->the", qf, kv.astype(BF), preferred_element_type=F32)
        den = den + jnp.sum(qf.astype(F32) * ks[:, None], axis=(0, 3))
        inv = 1.0 / (den + 1.0)
        atts.append((num * inv[:, :, None]).astype(BF).reshape(rows, -1))
        dens.append(jnp.broadcast_to(inv[:, :, None], num.shape).reshape(rows, -1))
    return jnp.concatenate(atts), jnp.concatenate(dens)


def state_grad(mixed, gatt, att, inv, info, rows):
    out = []
    for b in range(2):
        rq, _, _, _, _ = qkv_of(mixed, b, rows)
        gnum = heads_of(gatt, b, rows) * heads_of(inv, b, rows)
        e = jnp.sum(gnum * heads_of(att, b, rows).astype(F32), axis=2)
        f = jnp.stack([info["fbcos"][b], info["fbsin"][b]])
        qf = (f[:, :, None, None] * rq[None]).astype(BF)
        gkv = jnp.einsum("stha,the->shae", qf, gnum.astype(BF), preferred_element_type=F32)
        gks = -jnp.sum(qf.astype(F32) * e[None, :, :, None], axis=1)
        out.append(pack_state(gkv, gks))
    return jnp.stack(out)


def attend_back(mixed, gatt, att, inv, state, gstate, info, rows):
    out = []
    for b in range(2):
        rq, rk, v, q, k = qkv_of(mixed, b, rows)
        gnum = heads_of(gatt, b, rows) * heads_of(inv, b, rows)
        e = jnp.sum(gnum * heads_of(att, b, rows).astype(F32), axis=2)
        gn, vb, rqb, rkb = gnum.astype(BF), v.astype(BF), rq.astype(BF), rk.astype(BF)
        s = jnp.einsum("tha,uha->htu", rqb, rkb, preferred_element_type=F32)
        w = (s * info["mask"][b][None]).astype(BF)
        gw = jnp.einsum("the,uhe->htu", gn, vb, preferred_element_type=F32) - e.T[:, :, None]
        gs = (gw * info["mask"][b][None]).astype(BF)
        gq = jnp.einsum("htu,uha->tha", gs, rkb, preferred_element_type=F32)
        gk = jnp.einsum("htu,tha->uha", gs, rqb, preferred_element_type=F32)
        gv = jnp.einsum("htu,the->uhe", w, gn, preferred_element_type=F32)
        kv, ks = unpack_state(state[b])
        f = jnp.stack([info["fbcos"][b], info["fbsin"][b]])
        gqf = jnp.einsum("the,shae->stha", gn, kv.astype(BF), preferred_element_type=F32)
        gqf = gqf - e[None, :, :, None] * ks[:, None]
        gq = gq + jnp.sum(f[:, :, None, None] * gqf, axis=0)
        gkv, gks = unpack_state(gstate[b])
        m = jnp.stack([info["memcos"][b], info["memsin"][b]])
        gkf = jnp.einsum("uhe,shae->suha", vb, gkv.astype(BF), preferred_element_type=F32) + gks[:, None]
        gk = gk + jnp.sum(m[:, :, None, None] * gkf, axis=0)
        kf = (m[:, :, None, None] * rk[None]).astype(BF)
        gv = gv + jnp.einsum("suha,shae->uhe", kf, gkv.astype(BF), preferred_element_type=F32)
        gq = jnp.where(q > 0, gq, 0.0)
        gk = jnp.where(k > 0, gk, 0.0)
        out.append(jnp.concatenate([g.reshape(rows, -1) for g in (gq, gk, gv)], axis=1))
    return jnp.concatenate(out).astype(BF)


def regroup(states, mask, roll):
    own, other = states
    if mask & 1:
        own, other = other, own
    if roll is True:
        return jnp.roll(own, HD, axis=-1), jnp.roll(other, HD, axis=-1)
    if roll is False:
        return own, other
    return tuple(jnp.where(roll, jnp.roll(x, HD, axis=-1), x) for x in (own, other))


def exchange(states, shift, roll, flags):
    first = regroup([shift(x, 1) for x in states], 1, roll)
    second = regroup([shift(x, 2) for x in states], 2, True)
    scale = [f.astype(F32)[:, None, None, None] for f in flags]
    return [
        (a.astype(F32) * scale[0] + b.astype(F32) * scale[1]).astype(BF)
        for a, b in zip(first, second)
    ]


def shards(
    layer_input,
    doc_lengths,
    ln1_gain,
    ln1_bias,
    qkv_weight,
    out_weight,
    ln2_gain,
    ln2_bias,
    in_weight,
    down_weight,
    cotangent,
):
    batches, rows, width = layer_input.shape
    layers = qkv_weight.shape[0]
    n_dp = lax.axis_size("dp")
    d, h = lax.axis_index("dp"), lax.axis_index("head")
    block = width // n_dp
    groups = xor_groups(n_dp)
    order = block_order(groups)
    tokens = batches * rows

    first_row = h * rows
    info = {k: [] for k in ("memcos", "memsin", "fbcos", "fbsin", "mask")}
    from1, from2, to1, to2 = [], [], [], []
    for b in range(batches):
        lengths = doc_lengths[b]
        position = first_row + jnp.arange(rows, dtype=jnp.int32)
        doc, start, size = places(lengths, position)
        angle = math.pi / 2 * (position - start).astype(F32) / size.astype(F32)
        cos, sin = jnp.cos(angle), jnp.sin(angle)
        edges = jnp.stack(
            [first_row - rows - 1, first_row - 1, first_row, first_row + rows - 1, first_row + rows, first_row + 2 * rows]
        )
        at, _, _ = places(lengths, edges)
        from1.append((h >= 1) & (at[1] == at[2]))
        from2.append((h >= 2) & (at[0] == at[2]))
        to1.append((h <= 2) & (at[3] == at[4]))
        to2.append((h <= 1) & (at[3] == at[5]))
        fb = (doc == at[2]).astype(F32)
        mem = (doc == at[3]).astype(F32)
        same = (doc[:, None] == doc[None, :]) & (position[:, None] >= position[None, :])
        info["mask"].append(
            jnp.where(same, cos[:, None] * cos[None, :] + sin[:, None] * sin[None, :], 0.0)
        )
        for name, weight in (("mem", mem), ("fb", fb)):
            info[name + "cos"].append(weight * cos)
            info[name + "sin"].append(weight * sin)
    from1, from2, to1, to2 = [jnp.stack(f) for f in (from1, from2, to1, to2)]

    target = jnp.arange(width)
    source = (jnp.array(order)[target // block] ^ d) * block + target % block
    permutation = (jnp.arange(width)[:, None] == source[None, :]).astype(BF)
    x = dot(layer_input.reshape(tokens, width), permutation)
    cot = dot(cotangent.reshape(tokens, width), permutation)

    params = jnp.concatenate([ln1_gain, ln1_bias, ln2_gain, ln2_bias], axis=0)[None]
    for masks in groups:
        params = spread(params, "dp", masks, 0)
    params = params.transpose(1, 0, 2).reshape(4, layers, width).astype(F32)

    weights = []
    for l in range(layers):
        qkvo = jnp.concatenate([qkv_weight[l], out_weight[l].T], axis=1)
        one = gather(qkvo, groups, pair_columns, "x")
        two = gather(in_weight[l], groups, plain_columns, "y")
        three = gather(down_weight[l].T, groups, plain_columns, "x")
        weights.append((one, two, three))

    saved = []
    stream = x
    q3 = 3 * 6 * HD
    for l in range(layers):
        qkvo, w_in, w_down = weights[l]
        w_qkv = [w[:, :q3] for w in qkvo]
        w_out = [w[:, q3:] for w in qkvo]
        normed1, stats1 = norm(stream, params[0, l], params[1, l])
        mixed = [dot(normed1, w).astype(BF) for w in w_qkv]
        states = [local_state(m, info, rows) for m in mixed]
        state = exchange(states, forward_shift, h == 2, (from1, from2))
        att, inv = zip(*[attend(m, s, info, rows) for m, s in zip(mixed, state)])
        mid = stream + sum(dot_t(a, w) for a, w in zip(att, w_out))
        normed2, stats2 = norm(mid, params[2, l], params[3, l])
        act, slope = zip(*[gelu_and_slope(dot(normed2, w)) for w in w_in])
        out = mid + sum(dot_t(a, w) for a, w in zip(act, w_down))
        saved.append((stream, normed1, stats1, mixed, state, att, inv, mid, normed2, stats2, act, slope, w_qkv, w_out, w_in, w_down))
        stream = out

    layer_output = dot_t(stream.astype(BF), permutation).astype(BF).reshape(layer_input.shape)

    grad = cot
    grads = [None] * layers
    norm_grads = [None] * layers
    for l in reversed(range(layers)):
        (stream, normed1, stats1, mixed, state, att, inv, mid, normed2, stats2, act, slope, w_qkv, w_out, w_in, w_down) = saved[l]
        low = grad.astype(BF)
        down_g = reduce_scatter(t_dot(low, act[0]), t_dot(low, act[1]), groups, split_plain, "x")
        gpre = [(dot(low, w) * s.astype(F32)).astype(BF) for w, s in zip(w_down, slope)]
        in_g = reduce_scatter(t_dot(normed2, gpre[0]), t_dot(normed2, gpre[1]), groups, split_plain, "y")
        gn2 = sum(dot_t(g, w) for g, w in zip(gpre, w_in))
        back, gain2_g, bias2_g = norm_back(mid, stats2, params[2, l], gn2)
        grad = grad + back
        low = grad.astype(BF)
        out_g = reduce_scatter(t_dot(low, att[0]), t_dot(low, att[1]), groups, split_pairs, "x")
        gatt = [dot(low, w) for w in w_out]
        gstates = [state_grad(m, g, a, i, info, rows) for m, g, a, i in zip(mixed, gatt, att, inv)]
        gstate = exchange(gstates, backward_shift, h == 1, (to1, to2))
        gmixed = [
            attend_back(m, g, a, i, s, gs, info, rows)
            for m, g, a, i, s, gs in zip(mixed, gatt, att, inv, state, gstate)
        ]
        qkv_g = reduce_scatter(t_dot(normed1, gmixed[0]), t_dot(normed1, gmixed[1]), groups, split_pairs, "y")
        gn1 = sum(dot_t(g, w) for g, w in zip(gmixed, w_qkv))
        back, gain1_g, bias1_g = norm_back(stream, stats1, params[0, l], gn1)
        grad = grad + back
        grads[l] = (qkv_g, out_g.T, in_g, down_g.T)
        norm_grads[l] = (gain1_g, bias1_g, gain2_g, bias2_g)

    high = lax.reduce_precision(grad, 8, 7)
    input_grad = dot_t(high.astype(BF), permutation) + dot_t((grad - high).astype(BF), permutation)
    input_grad = input_grad.reshape(layer_input.shape)

    small = jnp.stack([norm_grads[l][i] for i in range(4) for l in range(layers)])
    small = small + swap(small, "head", 1)
    small = small + swap(small, "head", 2)
    small = small.reshape(4 * layers, n_dp, block).transpose(1, 0, 2)
    for masks in groups[::-1]:
        count = small.shape[0] // (len(masks) + 1)
        total = small[:count]
        for j, m in enumerate(masks):
            total = total + swap(small[(j + 1) * count : (j + 2) * count], "dp", m)
        small = total
    part = block // lax.axis_size("head")
    small = lax.dynamic_slice_in_dim(small.reshape(4, layers, block), h * part, part, 2)

    qkv_grad, out_grad, in_grad, down_grad = [jnp.stack([grads[l][i] for l in range(layers)]) for i in range(4)]
    return (
        layer_output,
        input_grad,
        small[0],
        small[1],
        qkv_grad,
        out_grad,
        small[2],
        small[3],
        in_grad,
        down_grad,
    )


def solution(mesh):
    in_specs = (
        P("dp", "head", None),
        P("dp", None),
        P(None, "dp"),
        P(None, "dp"),
        P(None, "dp", "head"),
        P(None, "head", "dp"),
        P(None, "dp"),
        P(None, "dp"),
        P(None, "dp", "head"),
        P(None, "head", "dp"),
        P("dp", "head", None),
    )
    out_specs = (
        P("dp", "head", None),
        P("dp", "head", None),
        P(None, ("dp", "head")),
        P(None, ("dp", "head")),
        P(None, "dp", "head"),
        P(None, "head", "dp"),
        P(None, ("dp", "head")),
        P(None, ("dp", "head")),
        P(None, "dp", "head"),
        P(None, "head", "dp"),
    )
    return jax.shard_map(shards, mesh=mesh, in_specs=in_specs, out_specs=out_specs, check_vma=False)
```

```python
from functools import partial
import math

import jax
import jax.numpy as jnp
from jax import lax
from jax.experimental import pallas as pl
from jax.experimental.pallas import tpu as pltpu
from jax.sharding import PartitionSpec as P

HD = 64
ROW = 2048
NORM_EPS = 1e-05
BF = jnp.bfloat16
F32 = jnp.float32


def xor_groups(n):
    groups, span = [[1]], 2
    while span < n:
        radix = min(4, n // span)
        groups.append([span * k for k in range(1, radix)])
        span *= radix
    return groups[::-1]


def swap(x, axis, mask):
    n = lax.axis_size(axis)
    return lax.ppermute(x, axis, [(i, i ^ mask) for i in range(n)])


def forward_shift(x, by):
    n = lax.axis_size("head")
    return lax.ppermute(x, "head", [(i, i + by) for i in range(n - by)])


def backward_shift(x, by):
    n = lax.axis_size("head")
    return lax.ppermute(x, "head", [(i + by, i) for i in range(n - by)])


def block_order(groups):
    order = [0]
    for masks in groups:
        order = order + [r ^ m for m in masks for r in order]
    return order


def spread(x, axis, masks, dim):
    return jnp.concatenate([x] + [swap(x, axis, m) for m in masks], axis=dim)


def pair_columns(own, other):
    heads = own.shape[1] // (4 * HD)
    pieces = []
    for part, j in [(part, j) for j in range(heads) for part in range(3)] + [(3, j) for j in range(heads)]:
        at = (part * heads + j) * HD
        pieces += [own[:, at : at + HD], other[:, at : at + HD]]
    return jnp.concatenate(pieces, axis=1)


def split_pairs(parts, x):
    heads = x.shape[1] // (2 * HD * parts)
    starts = [(j * parts + part) * 2 * HD for part in range(parts) for j in range(heads)]
    return tuple(
        jnp.concatenate([x[:, at + side : at + side + HD] for at in starts], axis=1) for side in (0, HD)
    )


def split_plain(x):
    c = x.shape[1] // 2
    return x[:, :c], x[:, c:]


class Transfers:
    def __init__(self, steps):
        self.steps, self.coming, self.result = steps, None, None
        self.wanted = next(steps)

    def give(self, arrived):
        try:
            self.wanted = self.steps.send(arrived)
        except StopIteration as end:
            self.wanted, self.result = [], end.value


def finish(value, chains):
    while True:
        chains = [chain for chain in chains if chain.result is None]
        if not chains:
            return value
        value = advance(value, *chains)


def shift_steps(state, shift):
    arrived = yield [(state, lambda array: shift(array, 1)), (state, lambda array: shift(array, 2))]
    return arrived


def together(values):
    return lax.optimization_barrier(values)


def start(*chains):
    for chain in chains:
        chain.coming = [exchange(array) for array, exchange in chain.wanted]


def advance(value, *chains):
    value, arrived = together((value, [chain.coming for chain in chains]))
    for chain, pieces in zip(chains, arrived):
        chain.give(pieces)
    value, sends = together((value, [[array for array, _ in chain.wanted] for chain in chains]))
    for chain, arrays in zip(chains, sends):
        chain.coming = [exchange(array) for array, (_, exchange) in zip(arrays, chain.wanted)]
    return value


def to(axis, mask):
    return lambda array: swap(array, axis, mask)


def spread_steps(x, masks):
    arrived = yield [(x, to("dp", m)) for m in masks]
    return jnp.concatenate([x] + arrived, axis=0)


def outer_steps(x, groups):
    for masks in groups[:-1]:
        x = yield from spread_steps(x, masks)
    return x


def heads_steps(shard, groups):
    x = yield from outer_steps(shard, groups)
    masks = groups[-1]
    c = x.shape[1] // 2
    qk, vo = x[:, :c], x[:, c:]
    arrived = yield [(qk, to("dp", m)) for m in masks] + [(vo, to("head", 2))]
    qk = jnp.concatenate([qk] + arrived[:-1], axis=0)
    vo = jnp.concatenate([vo, arrived[-1]], axis=1)
    arrived = yield [(qk, to("head", 2))] + [(vo, to("dp", m)) for m in masks]
    vo = jnp.concatenate([vo] + arrived[1:], axis=0)
    own = jnp.concatenate([qk, vo[:, :c]], axis=1)
    other = jnp.concatenate([arrived[0], vo[:, c:]], axis=1)
    half = pair_columns(own, other)
    arrived = yield [(half, to("head", 1))]
    return half, arrived[0]


def hidden_steps(shard, groups):
    x = yield from outer_steps(shard, groups)
    masks = groups[-1]
    c = x.shape[1] // 2
    up, down = x[:, :c], x[:, c:]
    arrived = yield [(up, to("dp", m)) for m in masks] + [(down, to("head", 2))]
    up = jnp.concatenate([up] + arrived[:-1], axis=0)
    down = jnp.concatenate([down, arrived[-1]], axis=1)
    arrived = yield [(up, to("head", 2))] + [(down, to("dp", m)) for m in masks]
    up = jnp.concatenate([up, arrived[0]], axis=1)
    down = jnp.concatenate([down] + arrived[1:], axis=0)
    arrived = yield [(up, to("head", 1)), (down, to("head", 1))]
    return (up, arrived[0]), (down, arrived[1])


def row_steps(x, masks):
    rows = x.shape[0] // (len(masks) + 1)
    arrived = yield [(x[(j + 1) * rows : (j + 2) * rows].astype(BF), to("dp", m)) for j, m in enumerate(masks)]
    return x[:rows].astype(F32) + sum(piece.astype(F32) for piece in arrived)


def sum_steps(left, right, groups, split, first):
    c = right.shape[1] // 2
    arrived = yield [(t_dot(left, right[:, c:]).astype(BF), to("head", 1))]
    total = t_dot(left, right[:, :c]) + arrived[0].astype(F32)
    rest = groups[::-1]
    if first == "y":
        total = yield from row_steps(total, rest[0])
        rest = rest[1:]
    keep, send = split(total)
    arrived = yield [(send.astype(BF), to("head", 2))]
    total = keep + arrived[0].astype(F32)
    for masks in rest:
        total = yield from row_steps(total, masks)
    return total


def dot(a, b):
    return lax.dot_general(a, b, (((1,), (0,)), ((), ())), preferred_element_type=F32)


def dot_t(a, b):
    return lax.dot_general(a, b, (((1,), (1,)), ((), ())), preferred_element_type=F32)


def t_dot(a, b):
    return lax.dot_general(a, b, (((0,), (0,)), ((), ())), preferred_element_type=F32)


def places(lengths, position):
    n = lengths.shape[0]
    upto = jnp.arange(n)[:, None] <= jnp.arange(n)[None, :]
    ends = jnp.sum(jnp.where(upto, lengths[:, None], 0), axis=0)
    passed = (position[:, None] >= ends[None, :]).astype(jnp.int32)
    doc = jnp.sum(passed, axis=1)
    start = jnp.sum(passed * lengths[None, :], axis=1)
    here = (doc[:, None] == jnp.arange(n)[None, :]).astype(jnp.int32)
    size = jnp.sum(here * lengths[None, :], axis=1)
    return doc, start, size


STATE_ROWS = 144
PAIR = 2 * HD
QKV = 3 * PAIR
VMEM_LIMIT = 56 * 2**20


def run(kernel, grid, ins, outs, scratch=(), flops=0, size=0, name=None):
    in_specs, arrays = [], []
    for array, block, index in ins:
        arrays.append(array)
        if block is None:
            in_specs.append(pl.BlockSpec(memory_space=index))
        else:
            in_specs.append(pl.BlockSpec(block, index))
    return pl.pallas_call(
        kernel,
        grid=grid,
        in_specs=in_specs,
        out_specs=[pl.BlockSpec(block, index) for _, _, block, index in outs],
        out_shape=[jax.ShapeDtypeStruct(shape, dtype) for shape, dtype, _, _ in outs],
        scratch_shapes=list(scratch),
        compiler_params=pltpu.CompilerParams(
            dimension_semantics=("arbitrary",) * len(grid), vmem_limit_bytes=VMEM_LIMIT
        ),
        cost_estimate=pl.CostEstimate(flops=int(flops), bytes_accessed=int(size), transcendentals=0),
        name=name,
    )(*arrays)


def low_lanes(shape):
    return lax.broadcasted_iota(jnp.int32, shape, 1) < HD


def relu(x):
    return jnp.maximum(x, jnp.zeros_like(x))


def moments(x):
    mean = jnp.mean(x, axis=-1, keepdims=True)
    centred = x - mean
    rstd = lax.rsqrt(jnp.mean(centred * centred, axis=-1, keepdims=True) + NORM_EPS)
    return centred * rstd, rstd


def project_kernel(row, x_ref, par_ref, own_ref, other_ref, normed_ref, mixed_ref):
    xhat, _ = moments(x_ref[...])
    normed = (xhat * par_ref[row : row + 1, :] + par_ref[row + 2 : row + 3, :]).astype(BF)
    normed_ref[...] = normed
    half = own_ref.shape[1]
    mixed_ref[:, :half] = dot(normed, own_ref[...]).astype(BF)
    mixed_ref[:, half:] = dot(normed, other_ref[...]).astype(BF)


def project(x, params, row, own, other):
    tokens, width = x.shape
    half = 3 * width // 2
    rows = min(256, tokens)
    return run(
        partial(project_kernel, row),
        (tokens // rows,),
        [
            (x, (rows, width), lambda i: (i, 0)),
            (params, params.shape, lambda i: (0, 0)),
            (own, (width, half), lambda i: (0, 0)),
            (other, (width, half), lambda i: (0, 0)),
        ],
        [
            ((tokens, width), BF, (rows, width), lambda i: (i, 0)),
            ((tokens, 2 * half), BF, (rows, 2 * half), lambda i: (i, 0)),
        ],
        flops=2 * tokens * width * 2 * half,
        size=tokens * width * 6 + tokens * half * 4 + width * half * 4,
        name="project",
    )


def packed(c, s, c_sum, s_sum):
    lo = low_lanes((HD, PAIR))
    first = jnp.where(lo, c[:HD], c[HD:])
    second = jnp.where(lo, s[:HD], s[HD:])
    at = lax.broadcasted_iota(jnp.int32, (STATE_ROWS - PAIR, PAIR), 0)
    sums = jnp.where(at == 0, c_sum, jnp.where(at == 1, s_sum, 0.0))
    return jnp.concatenate([first, second, sums], axis=0).astype(BF)


def unpacked(st):
    lo = low_lanes((HD, PAIR))
    both = []
    for at in (0, HD):
        x = st[at : at + HD]
        both.append(jnp.concatenate([jnp.where(lo, x, 0.0), jnp.where(lo, 0.0, x)], axis=0))
    return both[0], both[1], st[PAIR : PAIR + 1], st[PAIR + 1 : PAIR + 2]


def received(near_ref, far_ref, flag_ref, b):
    near = near_ref[0, 0].astype(F32)
    far = far_ref[0, 0].astype(F32)
    return (
        near * flag_ref[b, 0]
        + pltpu.roll(near, HD, 1) * flag_ref[b, 1]
        + pltpu.roll(far, HD, 1) * flag_ref[b, 2]
    )


def state_kernel(col_ref, mixed_ref, out_ref):
    k = relu(mixed_ref[:, PAIR : 2 * PAIR]).astype(F32)
    v = mixed_ref[:, 2 * PAIR :]
    kc = (k * col_ref[:, 2:3]).astype(BF)
    ks = (k * col_ref[:, 3:4]).astype(BF)
    out_ref[0, 0] = packed(
        t_dot(kc, v),
        t_dot(ks, v),
        jnp.sum(kc.astype(F32), axis=0, keepdims=True),
        jnp.sum(ks.astype(F32), axis=0, keepdims=True),
    )


def pair_grid(mixed, rows):
    tokens, width = mixed.shape
    return (tokens // rows, width // QKV)


def local_state(mixed, col, rows):
    grid = pair_grid(mixed, rows)
    return run(
        state_kernel,
        grid,
        [
            (col, (rows, col.shape[1]), lambda b, p: (b, 0)),
            (mixed, (rows, QKV), lambda b, p: (b, p)),
        ],
        [(grid + (STATE_ROWS, PAIR), BF, (1, 1, STATE_ROWS, PAIR), lambda b, p: (b, p, 0, 0))],
        flops=4 * mixed.shape[0] * mixed.shape[1] * PAIR,
        size=mixed.size * 2,
        name="local_state",
    )[0]


def mask_of(col_ref, row_ref):
    rows = col_ref.shape[0]
    shape = (rows, rows)
    t = lax.broadcasted_iota(jnp.int32, shape, 0)
    u = lax.broadcasted_iota(jnp.int32, shape, 1)
    cosine = col_ref[:, 4:5] * row_ref[0:1, :] + col_ref[:, 5:6] * row_ref[1:2, :]
    same = col_ref[:, 6:7] == row_ref[2:3, :]
    return cosine, same, t, u


def attend_kernel(flag_ref, col_ref, row_ref, mixed_ref, near_ref, far_ref, att_ref, inv_ref, mask_ref):
    b, p = pl.program_id(0), pl.program_id(1)
    rows = mixed_ref.shape[0]

    @pl.when(p == 0)
    def _():
        cosine, same, t, u = mask_of(col_ref, row_ref)
        mask_ref[...] = jnp.where(same & (t >= u), cosine, 0.0)

    c, s, c_sum, s_sum = unpacked(received(near_ref, far_ref, flag_ref, b))
    q, k, v = [relu(mixed_ref[:, i * PAIR : (i + 1) * PAIR]) if i < 2 else mixed_ref[:, 2 * PAIR :] for i in range(3)]
    lo = low_lanes((rows, PAIR))
    qf = q.astype(F32)
    qc, qs = qf * col_ref[:, 0:1], qf * col_ref[:, 1:2]
    inter = dot(jnp.concatenate([qc, qs], axis=1).astype(BF), jnp.concatenate([c, s], axis=0).astype(BF))
    ones = jnp.where(
        (lax.broadcasted_iota(jnp.int32, (PAIR, PAIR), 0) < HD) == low_lanes((PAIR, PAIR)), 1.0, 0.0
    ).astype(BF)
    inter_den = dot((qc * c_sum + qs * s_sum).astype(BF), ones)
    zero = jnp.zeros_like(q)
    q_of = [jnp.where(lo, q, zero), jnp.where(lo, zero, q)]
    v_one = jnp.concatenate([v, jnp.ones_like(v)], axis=1)
    step = min(256, rows)
    for at in range(0, rows, step):
        end = at + step
        here = slice(at, end)
        mask = mask_ref[here, :end]
        parts = []
        for head in range(2):
            w = (dot_t(q_of[head][here], k[:end]) * mask).astype(BF)
            parts.append(dot(w, v_one[:end]))
        pick = low_lanes((step, PAIR))
        num = jnp.where(pick, parts[0][:, :PAIR], parts[1][:, :PAIR]) + inter[here]
        den = jnp.where(pick, parts[0][:, PAIR:], parts[1][:, PAIR:]) + inter_den[here]
        inv = 1.0 / (den + 1.0)
        att_ref[here, :] = (num * inv).astype(BF)
        inv_ref[here, :] = inv


def attend(mixed, near, far, flags, col, row, rows):
    grid = pair_grid(mixed, rows)
    tokens = mixed.shape[0]
    pairs = grid[1]
    width = pairs * PAIR
    half = pairs // 2
    return run(
        attend_kernel,
        grid,
        [
            (flags, None, pltpu.SMEM),
            (col, (rows, col.shape[1]), lambda b, p: (b, 0)),
            (row, (row.shape[0], rows), lambda b, p: (0, b)),
            (mixed, (rows, QKV), lambda b, p: (b, p)),
            (near, (1, 1, STATE_ROWS, PAIR), lambda b, p: (b, lax.rem(p + half, pairs), 0, 0)),
            (far, (1, 1, STATE_ROWS, PAIR), lambda b, p: (b, p, 0, 0)),
        ],
        [
            ((tokens, width), BF, (rows, PAIR), lambda b, p: (b, p)),
            ((tokens, width), F32, (rows, PAIR), lambda b, p: (b, p)),
        ],
        scratch=[pltpu.VMEM((rows, rows), F32)],
        flops=2 * tokens * rows * pairs * 2 * 256,
        size=mixed.size * 2 + tokens * width * 6,
        name="attend",
    )


def gelu_and_slope(x):
    c = math.sqrt(2.0 / math.pi)
    k = 0.044715 * c
    x2 = x * x
    half = 0.5 + 0.5 * jnp.tanh(x * (c + k * x2))
    act = x * half
    slope = half + act * (1.0 - half) * (2.0 * c + (6.0 * k) * x2)
    return act.astype(BF), slope.astype(BF)


def hidden_kernel(
    row, x_ref, par_ref, att_ref, oo_ref, ox_ref, io_ref, ix_ref, do_ref, dx_ref,
    mid_ref, normed_ref, act_ref, slope_ref, out_ref,
):
    step = pl.program_id(0)
    tokens = x_ref.shape[0]
    rows = min(256, tokens)
    half = oo_ref.shape[1]

    @pl.when(step == 0)
    def _():
        @pl.loop(0, tokens // rows)
        def _(i):
            here = pl.ds(i * rows, rows)
            mid = x_ref[here, :] + dot_t(att_ref[here, :half], oo_ref[...]) + dot_t(att_ref[here, half:], ox_ref[...])
            mid_ref[here, :] = mid
            xhat, _ = moments(mid)
            normed_ref[here, :] = (xhat * par_ref[row : row + 1, :] + par_ref[row + 2 : row + 3, :]).astype(BF)
            out_ref[here, :] = mid

    def part(in_ref, down_ref):
        @pl.loop(0, tokens // rows)
        def _(i):
            here = pl.ds(i * rows, rows)
            act, slope = gelu_and_slope(dot(normed_ref[here, :], in_ref[...]))
            act_ref[here, :] = act
            slope_ref[here, :] = slope
            out_ref[here, :] += dot_t(act, down_ref[...])

    last_own = pl.num_programs(0) // 2

    @pl.when(step < last_own)
    def _():
        part(io_ref, do_ref)

    @pl.when(step >= last_own)
    def _():
        part(ix_ref, dx_ref)


def own_step(n):
    return lambda i: (0, jnp.minimum(i, n - 1))


def other_step(n):
    return lambda i: (0, jnp.maximum(i - n, 0))


def hidden(x, params, row, att, w_att, w_in, w_down):
    tokens, width = x.shape
    units = 2 * w_in[0].shape[1]
    chunk = width
    n = units // chunk // 2
    o_at = w_att[0].shape[1] // (width // 2) - 1
    whole = lambda i: (0, 0)
    return run(
        partial(hidden_kernel, row),
        (2 * n,),
        [
            (x, (tokens, width), whole),
            (params, params.shape, whole),
            (att, (tokens, width), whole),
            (w_att[0], (width, width // 2), lambda i: (0, o_at)),
            (w_att[1], (width, width // 2), lambda i: (0, o_at)),
            (w_in[0], (width, chunk), own_step(n)),
            (w_in[1], (width, chunk), other_step(n)),
            (w_down[0], (width, chunk), own_step(n)),
            (w_down[1], (width, chunk), other_step(n)),
        ],
        [
            ((tokens, width), F32, (tokens, width), whole),
            ((tokens, width), BF, (tokens, width), whole),
            ((tokens, units), BF, (tokens, chunk), lambda i: (0, i)),
            ((tokens, units), BF, (tokens, chunk), lambda i: (0, i)),
            ((tokens, width), F32, (tokens, width), whole),
        ],
        flops=2 * tokens * width * (2 * units + width),
        size=tokens * width * 16 + tokens * units * 4 + width * units * 4,
        name="hidden",
    )


def hidden_back_kernel(
    row, g_ref, par_ref, mid_ref, slope_ref, io_ref, ix_ref, do_ref, dx_ref,
    gpre_ref, out_ref, norm_ref, low_ref, acc_ref,
):
    step = pl.program_id(0)
    tokens = g_ref.shape[0]
    rows = min(256, tokens)

    @pl.when(step == 0)
    def _():
        low_ref[...] = g_ref[...].astype(BF)
        acc_ref[...] = jnp.zeros_like(acc_ref)
        norm_ref[...] = jnp.zeros_like(norm_ref)

    def part(in_ref, down_ref):
        @pl.loop(0, tokens // rows)
        def _(i):
            here = pl.ds(i * rows, rows)
            gpre = (dot(low_ref[here, :], down_ref[...]) * slope_ref[here, :].astype(F32)).astype(BF)
            gpre_ref[here, :] = gpre
            acc_ref[here, :] += dot_t(gpre, in_ref[...])

    last_own = pl.num_programs(0) // 2

    @pl.when(step < last_own)
    def _():
        part(io_ref, do_ref)

    @pl.when(step >= last_own)
    def _():
        part(ix_ref, dx_ref)

    @pl.when(step == pl.num_programs(0) - 1)
    def _():
        @pl.loop(0, tokens // rows)
        def _(i):
            here = pl.ds(i * rows, rows)
            out_ref[here, :] = g_ref[here, :] + norm_gradient(
                acc_ref[here, :], mid_ref[here, :], par_ref[row : row + 1, :], norm_ref
            )


def norm_gradient(grad, stream, gain, norm_ref):
    xhat, rstd = moments(stream)
    gx = grad * xhat
    norm_ref[0:1, :] += jnp.sum(gx, axis=0, keepdims=True)
    norm_ref[1:2, :] += jnp.sum(grad, axis=0, keepdims=True)
    g = grad * gain
    return rstd * (
        g - jnp.mean(g, axis=-1, keepdims=True) - xhat * jnp.mean(gx * gain, axis=-1, keepdims=True)
    )


def hidden_back(grad, params, row, mid, slope, w_in, w_down):
    tokens, width = grad.shape
    units = slope.shape[1]
    chunk = width
    n = units // chunk // 2
    whole = lambda i: (0, 0)
    return run(
        partial(hidden_back_kernel, row),
        (2 * n,),
        [
            (grad, (tokens, width), whole),
            (params, params.shape, whole),
            (mid, (tokens, width), whole),
            (slope, (tokens, chunk), lambda i: (0, i)),
            (w_in[0], (width, chunk), own_step(n)),
            (w_in[1], (width, chunk), other_step(n)),
            (w_down[0], (width, chunk), own_step(n)),
            (w_down[1], (width, chunk), other_step(n)),
        ],
        [
            ((tokens, units), BF, (tokens, chunk), lambda i: (0, i)),
            ((tokens, width), F32, (tokens, width), whole),
            ((8, width), F32, (8, width), whole),
        ],
        scratch=[pltpu.VMEM((tokens, width), BF), pltpu.VMEM((tokens, width), F32)],
        flops=2 * tokens * width * 2 * units,
        size=tokens * width * 12 + tokens * units * 4 + width * units * 4,
        name="hidden_back",
    )


def head_ones():
    return jnp.where(
        (lax.broadcasted_iota(jnp.int32, (PAIR, PAIR), 0) < HD) == low_lanes((PAIR, PAIR)), 1.0, 0.0
    ).astype(BF)


def state_back_kernel(col_ref, g_ref, oo_ref, ox_ref, q_ref, att_ref, inv_ref, gn_ref, out_ref, low_ref):
    p = pl.program_id(1)

    @pl.when(p == 0)
    def _():
        low_ref[...] = g_ref[...].astype(BF)

    w = jnp.where(p < pl.num_programs(1) // 2, oo_ref[...], ox_ref[...])
    gn = (dot(low_ref[...], w) * inv_ref[...]).astype(BF)
    gn_ref[...] = gn
    e = dot((gn.astype(F32) * att_ref[...].astype(F32)).astype(BF), head_ones())
    q = relu(q_ref[...]).astype(F32)
    qc = (q * col_ref[:, 0:1]).astype(BF)
    qs = (q * col_ref[:, 1:2]).astype(BF)
    out_ref[0, 0] = packed(
        t_dot(qc, gn),
        t_dot(qs, gn),
        -jnp.sum(qc.astype(F32) * e, axis=0, keepdims=True),
        -jnp.sum(qs.astype(F32) * e, axis=0, keepdims=True),
    )


def state_back(grad, mixed, att, inv, w_att, col, rows):
    grid = pair_grid(mixed, rows)
    tokens, width = grad.shape
    pairs = grid[1]
    half = pairs // 2
    o_at = 3 * half
    return run(
        state_back_kernel,
        grid,
        [
            (col, (rows, col.shape[1]), lambda b, p: (b, 0)),
            (grad, (rows, width), lambda b, p: (b, 0)),
            (w_att[0], (width, PAIR), lambda b, p: (0, o_at + jnp.minimum(p, half - 1))),
            (w_att[1], (width, PAIR), lambda b, p: (0, o_at + jnp.maximum(p - half, 0))),
            (mixed, (rows, PAIR), lambda b, p: (b, 3 * p)),
            (att, (rows, PAIR), lambda b, p: (b, p)),
            (inv, (rows, PAIR), lambda b, p: (b, p)),
        ],
        [
            ((tokens, width), BF, (rows, PAIR), lambda b, p: (b, p)),
            (grid + (STATE_ROWS, PAIR), BF, (1, 1, STATE_ROWS, PAIR), lambda b, p: (b, p, 0, 0)),
        ],
        scratch=[pltpu.VMEM((rows, width), BF)],
        flops=2 * tokens * width * 2 * width,
        size=tokens * width * 14,
        name="state_back",
    )


def attend_back_kernel(
    flag_ref, back_flag_ref, col_ref, row_ref, mixed_ref, gn_ref, att_ref,
    near_ref, far_ref, gnear_ref, gfar_ref, out_ref, mask_ref, turned_ref,
):
    b, p = pl.program_id(0), pl.program_id(1)
    rows = mixed_ref.shape[0]

    @pl.when(p == 0)
    def _():
        cosine, same, t, u = mask_of(col_ref, row_ref)
        mask_ref[...] = jnp.where(same & (t >= u), cosine, 0.0)
        turned_ref[...] = jnp.where(same & (t <= u), cosine, 0.0)

    q = relu(mixed_ref[:, :PAIR])
    k = relu(mixed_ref[:, PAIR : 2 * PAIR])
    v = mixed_ref[:, 2 * PAIR :]
    gn = gn_ref[...]
    shape = (rows, PAIR)
    lo = low_lanes(shape)
    lane = lax.broadcasted_iota(jnp.int32, shape, 1)
    zero = jnp.zeros_like(q)
    e = dot((gn.astype(F32) * att_ref[...].astype(F32)).astype(BF), head_ones())
    v_one = jnp.concatenate([v, jnp.where(lane < 2, 1.0, 0.0).astype(BF)], axis=1)
    step = min(256, rows)
    gq_of, gk_of, gv_of = [], [], []
    for head in range(2):
        own = lo if head == 0 else ~lo
        k_own = jnp.where(own, k, zero)
        e_own = e if head == 0 else pltpu.roll(e, HD, 1)
        e_high = e_own.astype(BF)
        e_low = (e_own - e_high.astype(F32)).astype(BF)
        tail = jnp.where(lane == 0, -e_high, jnp.where(lane == 1, -e_low, zero))
        g_tail = jnp.concatenate([jnp.where(own, gn, zero), tail], axis=1)
        gq, gk, gv = [], [], []
        for at in range(0, rows, step):
            end = at + step
            gs = (dot_t(g_tail[at:end], v_one[:end]) * mask_ref[at:end, :end]).astype(BF)
            gq.append(dot(gs, k[:end]))
            turned = turned_ref[at:end, at:]
            w_t = (dot_t(k_own[at:end], q[at:]) * turned).astype(BF)
            gv.append(dot(w_t, gn[at:]))
            gs_t = (dot_t(v_one[at:end], g_tail[at:]) * turned).astype(BF)
            gk.append(dot(gs_t, q[at:]))
        gq_of.append(jnp.concatenate(gq, axis=0))
        gk_of.append(jnp.concatenate(gk, axis=0))
        gv_of.append(jnp.concatenate(gv, axis=0))

    c, s, c_sum, s_sum = unpacked(received(near_ref, far_ref, flag_ref, b))
    gc, gs, gc_sum, gs_sum = unpacked(received(gnear_ref, gfar_ref, back_flag_ref, b))
    gq = jnp.where(lo, gq_of[0], gq_of[1])
    gq += col_ref[:, 0:1] * (dot_t(gn, c.astype(BF)) - e * c_sum)
    gq += col_ref[:, 1:2] * (dot_t(gn, s.astype(BF)) - e * s_sum)
    gk = jnp.where(lo, gk_of[0], gk_of[1])
    gk += col_ref[:, 2:3] * (dot_t(v, gc.astype(BF)) + gc_sum)
    gk += col_ref[:, 3:4] * (dot_t(v, gs.astype(BF)) + gs_sum)
    kf = k.astype(F32)
    gv = jnp.where(lo, gv_of[0], gv_of[1])
    gv += dot((kf * col_ref[:, 2:3]).astype(BF), gc.astype(BF))
    gv += dot((kf * col_ref[:, 3:4]).astype(BF), gs.astype(BF))
    out_ref[:, :PAIR] = jnp.where(q > 0, gq, 0.0).astype(BF)
    out_ref[:, PAIR : 2 * PAIR] = jnp.where(k > 0, gk, 0.0).astype(BF)
    out_ref[:, 2 * PAIR :] = gv.astype(BF)


def attend_back(mixed, gn, att, near, far, gnear, gfar, flags, back_flags, col, row, rows):
    grid = pair_grid(mixed, rows)
    pairs = grid[1]
    half = pairs // 2
    state = (1, 1, STATE_ROWS, PAIR)
    direct = lambda b, p: (b, p, 0, 0)
    crossed = lambda b, p: (b, lax.rem(p + half, pairs), 0, 0)
    return run(
        attend_back_kernel,
        grid,
        [
            (flags, None, pltpu.SMEM),
            (back_flags, None, pltpu.SMEM),
            (col, (rows, col.shape[1]), lambda b, p: (b, 0)),
            (row, (row.shape[0], rows), lambda b, p: (0, b)),
            (mixed, (rows, QKV), lambda b, p: (b, p)),
            (gn, (rows, PAIR), lambda b, p: (b, p)),
            (att, (rows, PAIR), lambda b, p: (b, p)),
            (near, state, crossed),
            (far, state, direct),
            (gnear, state, crossed),
            (gfar, state, direct),
        ],
        [(mixed.shape, BF, (rows, QKV), lambda b, p: (b, p))],
        scratch=[pltpu.VMEM((rows, rows), F32), pltpu.VMEM((rows, rows), F32)],
        flops=6 * mixed.shape[0] * rows * pairs * 2 * 256,
        size=mixed.size * 4 + gn.size * 4,
        name="attend_back",
    )[0]


def project_back_kernel(row, gm_ref, own_ref, other_ref, x_ref, par_ref, g_ref, out_ref, norm_ref):
    @pl.when(pl.program_id(0) == 0)
    def _():
        norm_ref[...] = jnp.zeros_like(norm_ref)

    half = own_ref.shape[1]
    grad = dot_t(gm_ref[:, :half], own_ref[...]) + dot_t(gm_ref[:, half:], other_ref[...])
    out_ref[...] = g_ref[...] + norm_gradient(grad, x_ref[...], par_ref[row : row + 1, :], norm_ref)


def project_back(gmixed, own, other, x, params, row, grad):
    tokens, width = x.shape
    half = gmixed.shape[1] // 2
    rows = min(256, tokens)
    whole = lambda i: (0, 0)
    by_row = lambda i: (i, 0)
    return run(
        partial(project_back_kernel, row),
        (tokens // rows,),
        [
            (gmixed, (rows, 2 * half), by_row),
            (own, (width, half), whole),
            (other, (width, half), whole),
            (x, (rows, width), by_row),
            (params, params.shape, whole),
            (grad, (rows, width), by_row),
        ],
        [
            ((tokens, width), F32, (rows, width), by_row),
            ((8, width), F32, (8, width), whole),
        ],
        flops=2 * tokens * width * 2 * half,
        size=tokens * width * 12 + tokens * half * 4 + width * half * 4,
        name="project_back",
    )


def shards(
    layer_input,
    doc_lengths,
    ln1_gain,
    ln1_bias,
    qkv_weight,
    out_weight,
    ln2_gain,
    ln2_bias,
    in_weight,
    down_weight,
    cotangent,
):
    batches, rows, width = layer_input.shape
    layers = qkv_weight.shape[0]
    n_dp = lax.axis_size("dp")
    d, h = lax.axis_index("dp"), lax.axis_index("head")
    block = width // n_dp
    groups = xor_groups(n_dp)
    order = block_order(groups)
    tokens = batches * rows

    first_row = h * rows
    col, row, flags, back_flags = [], [], [], []
    for b in range(batches):
        lengths = doc_lengths[b]
        position = first_row + jnp.arange(rows, dtype=jnp.int32)
        doc, begin, size = places(lengths, position)
        angle = math.pi / 2 * (position - begin).astype(F32) / size.astype(F32)
        cos, sin = jnp.cos(angle), jnp.sin(angle)
        edges = first_row + jnp.array([-rows - 1, -1, 0, rows - 1, rows, 2 * rows], jnp.int32)
        at, _, _ = places(lengths, edges)
        first = (doc == at[2]).astype(F32)
        final = (doc == at[3]).astype(F32)
        place = doc.astype(F32)
        zero = jnp.zeros_like(cos)
        col.append(jnp.stack([first * cos, first * sin, final * cos, final * sin, cos, sin, place, zero], axis=1))
        row.append(jnp.stack([cos, sin, place, zero, zero, zero, zero, zero]))
        last = lax.axis_size("head") - 1
        near = (h >= 1) & (at[1] == at[2])
        far = (h >= 2) & (at[0] == at[2])
        flags.append(jnp.stack([near & (h != 2), near & (h == 2), far]))
        near = (h <= last - 1) & (at[3] == at[4])
        far = (h <= last - 2) & (at[3] == at[5])
        back_flags.append(jnp.stack([near & (h != 1), near & (h == 1), far]))
    col, row = jnp.concatenate(col), jnp.concatenate(row, axis=1)
    flags, back_flags = jnp.stack(flags).astype(F32), jnp.stack(back_flags).astype(F32)

    target = jnp.arange(width)
    source = (jnp.array(order)[target // block] ^ d) * block + target % block
    permutation = (jnp.arange(width)[:, None] == source[None, :]).astype(BF)
    x = dot(layer_input.reshape(tokens, width), permutation)
    cot = dot(cotangent.reshape(tokens, width), permutation)

    weights = []
    for l in range(layers):
        qkvo = jnp.concatenate([qkv_weight[l], out_weight[l].T], axis=1)
        updown = jnp.concatenate([in_weight[l], down_weight[l].T], axis=1)
        weights.append((Transfers(heads_steps(qkvo, groups)), Transfers(hidden_steps(updown, groups))))
    heads0, hidden0 = weights[0]
    start(heads0)

    params = jnp.concatenate([ln1_gain, ln1_bias, ln2_gain, ln2_bias], axis=0)[None]
    for masks in groups:
        params = spread(params, "dp", masks, 0)
    params = params.transpose(1, 0, 2).reshape(4 * layers, width).astype(F32)

    stream = x
    for _ in range(len(groups) - 2):
        stream = advance(stream, heads0)
    stream = advance(stream, heads0)
    start(hidden0)
    stream = advance(stream, heads0)
    stream = advance(stream, heads0)
    stream = advance(stream, heads0)
    for _ in range(len(groups) - 2):
        stream = advance(stream, hidden0)

    saved = []
    for l in range(layers):
        heads, units = weights[l]
        nheads, nunits = weights[l + 1] if l + 1 < layers else (None, None)
        w_att = heads.result
        if l == 0:
            stream = advance(stream, units)
        normed1, mixed = project(stream, params, l, *w_att)
        if nheads:
            start(nheads)
        mixed = advance(mixed, units)
        state = local_state(mixed, col, rows)
        states = Transfers(shift_steps(state, forward_shift))
        start(states)
        if nheads:
            for _ in range(len(groups) - 2):
                mixed = advance(mixed, nheads)
            mixed = advance(mixed, nheads)
            start(nunits)
        mixed = advance(mixed, states)
        near, far = states.result
        att, inv = attend(mixed, near, far, flags, col, row, rows)
        att = advance(att, units)
        if nheads:
            att = advance(att, nheads)
            for _ in range(len(groups) - 2):
                att = advance(att, nunits)
        att = advance(att, units)
        w_in, w_down = units.result
        mid, normed2, act, slope, out = hidden(stream, params, 2 * layers + l, att, w_att, w_in, w_down)
        saved.append((stream, normed1, mixed, near, far, att, inv, mid, normed2, act, slope, w_att, w_in, w_down))
        stream = out
        if nheads:
            stream = advance(stream, nheads, nunits)
            stream = advance(stream, nheads)

    layer_output = dot_t(stream.astype(BF), permutation).astype(BF).reshape(layer_input.shape)

    grad = cot
    sums = []
    norm_grads = [None] * layers
    for l in reversed(range(layers)):
        stream, normed1, mixed, near, far, att, inv, mid, normed2, act, slope, w_att, w_in, w_down = saved[l]
        previous = sums[-1] if sums else None
        down_g = Transfers(sum_steps(grad.astype(BF), act, groups, split_plain, "y"))
        start(down_g)
        gpre, grad, norm2_g = hidden_back(grad, params, 2 * layers + l, mid, slope, w_in, w_down)
        in_g = Transfers(sum_steps(normed2, gpre, groups, split_plain, "x"))
        start(in_g)
        grad = advance(grad, down_g)
        if previous:
            grad = advance(grad, *previous)
        gn, gstate = state_back(grad, mixed, att, inv, w_att, col, rows)
        gstates = Transfers(shift_steps(gstate, backward_shift))
        start(gstates)
        out_g = Transfers(sum_steps(grad.astype(BF), att, groups, partial(split_pairs, 1), "x"))
        start(out_g)
        gn = advance(gn, in_g)
        if previous:
            gn = advance(gn, previous[2], previous[3])
        gn = advance(gn, gstates)
        gnear, gfar = gstates.result
        gmixed = attend_back(mixed, gn, att, near, far, gnear, gfar, flags, back_flags, col, row, rows)
        gmixed = advance(gmixed, out_g, down_g, in_g)
        qkv_g = Transfers(sum_steps(normed1, gmixed, groups, partial(split_pairs, 3), "y"))
        start(qkv_g)
        if previous:
            gmixed = advance(gmixed, previous[3])
        grad, norm1_g = project_back(gmixed, *w_att, stream, params, l, grad)
        grad = advance(grad, qkv_g, out_g, down_g, in_g)
        sums.append((down_g, in_g, out_g, qkv_g))
        norm_grads[l] = (norm1_g[0], norm1_g[1], norm2_g[0], norm2_g[1])

    high = lax.reduce_precision(grad, 8, 7)
    input_grad = dot_t(high.astype(BF), permutation) + dot_t((grad - high).astype(BF), permutation)
    input_grad = input_grad.reshape(layer_input.shape)

    small = jnp.stack([norm_grads[l][i] for i in range(4) for l in range(layers)])
    small = small + swap(small, "head", 1)
    small = small + swap(small, "head", 2)
    small = small.reshape(4 * layers, n_dp, block).transpose(1, 0, 2)
    for masks in groups[::-1]:
        count = small.shape[0] // (len(masks) + 1)
        total = small[:count]
        for j, m in enumerate(masks):
            total = total + swap(small[(j + 1) * count : (j + 2) * count], "dp", m)
        small = total
    part = block // lax.axis_size("head")
    small = lax.dynamic_slice_in_dim(small.reshape(4, layers, block), h * part, part, 2)

    input_grad = finish(input_grad, [chain for layer in sums for chain in layer])
    sums = sums[::-1]
    down_grad = jnp.stack([s[0].result.T for s in sums])
    in_grad = jnp.stack([s[1].result for s in sums])
    out_grad = jnp.stack([s[2].result.T for s in sums])
    qkv_grad = jnp.stack([s[3].result for s in sums])
    return (
        layer_output,
        input_grad,
        small[0],
        small[1],
        qkv_grad,
        out_grad,
        small[2],
        small[3],
        in_grad,
        down_grad,
    )


def solution(mesh):
    in_specs = (
        P("dp", "head", None),
        P("dp", None),
        P(None, "dp"),
        P(None, "dp"),
        P(None, "dp", "head"),
        P(None, "head", "dp"),
        P(None, "dp"),
        P(None, "dp"),
        P(None, "dp", "head"),
        P(None, "head", "dp"),
        P("dp", "head", None),
    )
    out_specs = (
        P("dp", "head", None),
        P("dp", "head", None),
        P(None, ("dp", "head")),
        P(None, ("dp", "head")),
        P(None, "dp", "head"),
        P(None, "head", "dp"),
        P(None, ("dp", "head")),
        P(None, ("dp", "head")),
        P(None, "dp", "head"),
        P(None, "head", "dp"),
    )
    return jax.shard_map(shards, mesh=mesh, in_specs=in_specs, out_specs=out_specs, check_vma=False)
```

```python
from functools import partial
import math

import jax
import jax.numpy as jnp
from jax import lax
from jax.experimental import pallas as pl
from jax.experimental.pallas import tpu as pltpu
from jax.sharding import PartitionSpec as P

HD = 64
ROW = 2048
NORM_EPS = 1e-05
BF = jnp.bfloat16
F32 = jnp.float32


def xor_groups(n):
    groups, span = [[1]], 2
    while span < n:
        radix = min(4, n // span)
        groups.append([span * k for k in range(1, radix)])
        span *= radix
    return groups[::-1]


def swap(x, axis, mask):
    n = lax.axis_size(axis)
    return lax.ppermute(x, axis, [(i, i ^ mask) for i in range(n)])


def forward_shift(x, by):
    n = lax.axis_size("head")
    return lax.ppermute(x, "head", [(i, i + by) for i in range(n - by)])


def backward_shift(x, by):
    n = lax.axis_size("head")
    return lax.ppermute(x, "head", [(i + by, i) for i in range(n - by)])


def block_order(groups):
    order = [0]
    for masks in groups:
        order = order + [r ^ m for m in masks for r in order]
    return order


def spread(x, axis, masks, dim):
    return jnp.concatenate([x] + [swap(x, axis, m) for m in masks], axis=dim)


def pair_columns(own, other):
    heads = own.shape[1] // (4 * HD)
    pieces = []
    for part, j in [(part, j) for j in range(heads) for part in range(3)] + [(3, j) for j in range(heads)]:
        at = (part * heads + j) * HD
        pieces += [own[:, at : at + HD], other[:, at : at + HD]]
    return jnp.concatenate(pieces, axis=1)


class Transfers:
    def __init__(self, steps):
        self.steps, self.coming, self.result = steps, None, None
        self.wanted = next(steps)

    def give(self, arrived):
        try:
            self.wanted = self.steps.send(arrived)
        except StopIteration as end:
            self.wanted, self.result = [], end.value


def finish(value, chains):
    while True:
        chains = [chain for chain in chains if chain.result is None]
        if not chains:
            return value
        value = advance(value, *chains)


def shift_steps(state, shift):
    arrived = yield [(state, lambda array: shift(array, 1)), (state, lambda array: shift(array, 2))]
    return arrived


def together(values):
    return lax.optimization_barrier(values)


def start(*chains):
    for chain in chains:
        chain.coming = [exchange(array) for array, exchange in chain.wanted]


def advance(value, *chains):
    value, arrived = together((value, [chain.coming for chain in chains]))
    for chain, pieces in zip(chains, arrived):
        chain.give(pieces)
    value, sends = together((value, [[array for array, _ in chain.wanted] for chain in chains]))
    for chain, arrays in zip(chains, sends):
        chain.coming = [exchange(array) for array, (_, exchange) in zip(arrays, chain.wanted)]
    return value


def to(axis, mask):
    return lambda array: swap(array, axis, mask)


def spread_steps(x, masks):
    arrived = yield [(x, to("dp", m)) for m in masks]
    return jnp.concatenate([x] + arrived, axis=0)


def outer_steps(x, groups):
    for masks in groups[:-1]:
        x = yield from spread_steps(x, masks)
    return x


def heads_steps(shard, groups):
    x = yield from outer_steps(shard, groups)
    masks = groups[-1]
    c = x.shape[1] // 2
    qk, vo = x[:, :c], x[:, c:]
    arrived = yield [(qk, to("dp", m)) for m in masks] + [(vo, to("head", 2))]
    qk = jnp.concatenate([qk] + arrived[:-1], axis=0)
    vo = jnp.concatenate([vo, arrived[-1]], axis=1)
    arrived = yield [(qk, to("head", 2))] + [(vo, to("dp", m)) for m in masks]
    vo = jnp.concatenate([vo] + arrived[1:], axis=0)
    own = jnp.concatenate([qk, vo[:, :c]], axis=1)
    other = jnp.concatenate([arrived[0], vo[:, c:]], axis=1)
    half = pair_columns(own, other)
    arrived = yield [(half, to("head", 1))]
    return half, arrived[0]


def hidden_steps(shard, groups):
    x = yield from outer_steps(shard, groups)
    masks = groups[-1]
    c = x.shape[1] // 2
    up, down = x[:, :c], x[:, c:]
    arrived = yield [(up, to("dp", m)) for m in masks] + [(down, to("head", 2))]
    up = jnp.concatenate([up] + arrived[:-1], axis=0)
    down = jnp.concatenate([down, arrived[-1]], axis=1)
    arrived = yield [(up, to("head", 2))] + [(down, to("dp", m)) for m in masks]
    down = jnp.concatenate([down] + arrived[1:], axis=0)
    half = jnp.stack([jnp.stack([up, arrived[0]]), jnp.stack([down[:, :c], down[:, c:]])])
    arrived = yield [(half, to("head", 1))]
    return half, arrived[0]


def add(kept, *pieces):
    return (kept.astype(F32) + sum(piece.astype(F32) for piece in pieces)).astype(BF)


def last_rows(parts, groups):
    x = jnp.concatenate(parts, axis=1)
    for masks in groups[:-1][::-1]:
        rows = x.shape[0] // (len(masks) + 1)
        pieces = [x[j * rows : (j + 1) * rows] for j in range(len(masks) + 1)]
        arrived = yield [(piece, to("dp", m)) for piece, m in zip(pieces[1:], masks)]
        x = add(pieces[0], *arrived) if masks is not groups[0] else pieces[0].astype(F32) + sum(a.astype(F32) for a in arrived)
    return x


def sum_steps(other, join, split, groups):
    arrived = yield [(other, to("head", 1))]
    y_first, x_first = split(join(arrived[0]))
    (mask,) = groups[-1]
    rows = x_first.shape[1] // 2
    arrived = yield [(y_first[:, rows:], to("dp", mask)), (x_first[1], to("head", 2))]
    y_first = add(y_first[:, :rows], arrived[0])
    x_first = add(x_first[0], arrived[1])
    arrived = yield [(y_first[1], to("head", 2)), (x_first[rows:], to("dp", mask))]
    y_first = add(y_first[0], arrived[0])
    x_first = add(x_first[:rows], arrived[1])
    return (yield from last_rows([y_first, x_first], groups))


def dot(a, b):
    return lax.dot_general(a, b, (((1,), (0,)), ((), ())), preferred_element_type=F32)


def dot_t(a, b):
    return lax.dot_general(a, b, (((1,), (1,)), ((), ())), preferred_element_type=F32)


def t_dot(a, b):
    return lax.dot_general(a, b, (((0,), (0,)), ((), ())), preferred_element_type=F32)


def places(lengths, position):
    n = lengths.shape[0]
    upto = jnp.arange(n)[:, None] <= jnp.arange(n)[None, :]
    ends = jnp.sum(jnp.where(upto, lengths[:, None], 0), axis=0)
    passed = (position[:, None] >= ends[None, :]).astype(jnp.int32)
    doc = jnp.sum(passed, axis=1)
    start = jnp.sum(passed * lengths[None, :], axis=1)
    here = (doc[:, None] == jnp.arange(n)[None, :]).astype(jnp.int32)
    size = jnp.sum(here * lengths[None, :], axis=1)
    return doc, start, size


STATE_ROWS = 144
PAIR = 2 * HD
QKV = 3 * PAIR
VMEM_LIMIT = 60 * 2**20
EXPECTED_US = {
    "project": 10,
    "attend": 15,
    "hidden": 28,
    "hidden_back_other": 16,
    "hidden_back": 26,
    "attend_back": 28,
    "project_sums": 15,
    "project_back": 10,
}


def run(kernel, grid, ins, outs, scratch=(), name=None):
    in_specs, arrays = [], []
    for array, block, index in ins:
        arrays.append(array)
        if block is None:
            in_specs.append(pl.BlockSpec(memory_space=index))
        else:
            in_specs.append(pl.BlockSpec(block, index))
    return pl.pallas_call(
        kernel,
        grid=grid,
        in_specs=in_specs,
        out_specs=[
            pl.BlockSpec(memory_space=index) if block is None else pl.BlockSpec(block, index)
            for _, _, block, index in outs
        ],
        out_shape=[jax.ShapeDtypeStruct(shape, dtype) for shape, dtype, _, _ in outs],
        scratch_shapes=list(scratch),
        compiler_params=pltpu.CompilerParams(
            dimension_semantics=("arbitrary",) * len(grid), vmem_limit_bytes=VMEM_LIMIT
        ),
        cost_estimate=pl.CostEstimate(flops=EXPECTED_US[name] * 10**9, bytes_accessed=1000, transcendentals=0),
        name=name,
    )(*arrays)


def low_lanes(shape):
    return lax.broadcasted_iota(jnp.int32, shape, 1) < HD


def relu(x):
    return jnp.maximum(x, jnp.zeros_like(x))


def moments(x):
    mean = jnp.mean(x, axis=-1, keepdims=True)
    centred = x - mean
    rstd = lax.rsqrt(jnp.mean(centred * centred, axis=-1, keepdims=True) + NORM_EPS)
    return centred * rstd, rstd


def packed(c, s, c_sum, s_sum):
    lo = low_lanes((HD, PAIR))
    first = jnp.where(lo, c[:HD], c[HD:])
    second = jnp.where(lo, s[:HD], s[HD:])
    at = lax.broadcasted_iota(jnp.int32, (STATE_ROWS - PAIR, PAIR), 0)
    sums = jnp.where(at == 0, c_sum, jnp.where(at == 1, s_sum, 0.0))
    return jnp.concatenate([first, second, sums], axis=0).astype(BF)


def unpacked(st):
    lo = low_lanes((HD, PAIR))
    both = []
    for at in (0, HD):
        x = st[at : at + HD]
        both.append(jnp.concatenate([jnp.where(lo, x, 0.0), jnp.where(lo, 0.0, x)], axis=0))
    return both[0], both[1], st[PAIR : PAIR + 1], st[PAIR + 1 : PAIR + 2]


def received(near, far, flag_ref, b):
    near, far = near.astype(F32), far.astype(F32)
    return (
        near * flag_ref[b, 0]
        + pltpu.roll(near, HD, 1) * flag_ref[b, 1]
        + pltpu.roll(far, HD, 1) * flag_ref[b, 2]
    )


def project_kernel(row, x_ref, par_ref, col_ref, own_ref, other_ref, normed_ref, mixed_ref, state_ref):
    xhat, _ = moments(x_ref[...])
    normed = (xhat * par_ref[row : row + 1, :] + par_ref[row + 2 : row + 3, :]).astype(BF)
    normed_ref[...] = normed
    half = own_ref.shape[1]
    mixed_ref[:, :half] = dot(normed, own_ref[...]).astype(BF)
    mixed_ref[:, half:] = dot(normed, other_ref[...]).astype(BF)
    for p in range(2 * half // QKV):
        at = p * QKV
        k = relu(mixed_ref[:, at + PAIR : at + 2 * PAIR]).astype(F32)
        v = mixed_ref[:, at + 2 * PAIR : at + QKV]
        kc = (k * col_ref[:, 2:3]).astype(BF)
        ks = (k * col_ref[:, 3:4]).astype(BF)
        state_ref[0, p] = packed(
            t_dot(kc, v),
            t_dot(ks, v),
            jnp.sum(kc.astype(F32), axis=0, keepdims=True),
            jnp.sum(ks.astype(F32), axis=0, keepdims=True),
        )


def project(x, params, row, own, other, col, rows):
    tokens, width = x.shape
    half = 3 * width // 2
    pairs = 2 * half // QKV
    return run(
        partial(project_kernel, row),
        (tokens // rows,),
        [
            (x, (rows, width), lambda i: (i, 0)),
            (params, params.shape, lambda i: (0, 0)),
            (col, (rows, col.shape[1]), lambda i: (i, 0)),
            (own, (width, half), lambda i: (0, 0)),
            (other, (width, half), lambda i: (0, 0)),
        ],
        [
            ((tokens, width), BF, (rows, width), lambda i: (i, 0)),
            ((tokens, 2 * half), BF, (rows, 2 * half), lambda i: (i, 0)),
            ((tokens // rows, pairs, STATE_ROWS, PAIR), BF, (1, pairs, STATE_ROWS, PAIR), lambda i: (i, 0, 0, 0)),
        ],
        name="project",
    )


def pair_grid(mixed, rows):
    tokens, width = mixed.shape
    return (tokens // rows, width // QKV)


def mask_of(col_ref, row_ref):
    rows = col_ref.shape[0]
    shape = (rows, rows)
    t = lax.broadcasted_iota(jnp.int32, shape, 0)
    u = lax.broadcasted_iota(jnp.int32, shape, 1)
    cosine = col_ref[:, 4:5] * row_ref[0:1, :] + col_ref[:, 5:6] * row_ref[1:2, :]
    same = col_ref[:, 6:7] == row_ref[2:3, :]
    return cosine, same, t, u


def attend_kernel(col_ref, row_ref, mixed_ref, num_ref, den_ref, mask_ref):
    rows = mixed_ref.shape[0]

    @pl.when(pl.program_id(1) == 0)
    def _():
        cosine, same, t, u = mask_of(col_ref, row_ref)
        mask_ref[...] = jnp.where(same & (t >= u), cosine, 0.0)

    q, k, v = relu(mixed_ref[:, :PAIR]), relu(mixed_ref[:, PAIR : 2 * PAIR]), mixed_ref[:, 2 * PAIR :]
    lo = low_lanes((rows, PAIR))
    zero = jnp.zeros_like(q)
    q_of = [jnp.where(lo, q, zero), jnp.where(lo, zero, q)]
    v_one = jnp.concatenate([v, jnp.ones_like(v)], axis=1)
    step = min(256, rows)
    for at in range(0, rows, step):
        end = at + step
        here = slice(at, end)
        mask = mask_ref[here, :end]
        parts = []
        for head in range(2):
            w = (dot_t(q_of[head][here], k[:end]) * mask).astype(BF)
            parts.append(dot(w, v_one[:end]))
        pick = low_lanes((step, PAIR))
        num_ref[here, :] = jnp.where(pick, parts[0][:, :PAIR], parts[1][:, :PAIR])
        den_ref[here, :] = jnp.where(pick, parts[0][:, PAIR:], parts[1][:, PAIR:])


def attend(mixed, col, row, rows):
    grid = pair_grid(mixed, rows)
    tokens = mixed.shape[0]
    width = grid[1] * PAIR
    return run(
        attend_kernel,
        grid,
        [
            (col, (rows, col.shape[1]), lambda b, p: (b, 0)),
            (row, (row.shape[0], rows), lambda b, p: (0, b)),
            (mixed, (rows, QKV), lambda b, p: (b, p)),
        ],
        [
            ((tokens, width), F32, (rows, PAIR), lambda b, p: (b, p)),
            ((tokens, width), F32, (rows, PAIR), lambda b, p: (b, p)),
        ],
        scratch=[pltpu.VMEM((rows, rows), F32)],
        name="attend",
    )


def head_ones():
    return jnp.where(
        (lax.broadcasted_iota(jnp.int32, (PAIR, PAIR), 0) < HD) == low_lanes((PAIR, PAIR)), 1.0, 0.0
    ).astype(BF)


def gelu_and_slope(x):
    c = math.sqrt(2.0 / math.pi)
    k = 0.044715 * c
    x2 = x * x
    half = 0.5 + 0.5 * jnp.tanh(x * (c + k * x2))
    act = x * half
    slope = half + act * (1.0 - half) * (2.0 * c + (6.0 * k) * x2)
    return act.astype(BF), slope.astype(BF)


def copy(source, target, sem):
    made = pltpu.make_async_copy(source, target, sem)
    made.start()
    return made


def hidden_kernel(
    row, seq, flag_ref, par_ref, col_ref, near_ref, far_ref,
    x_hbm, num_hbm, den_hbm, mixed_hbm, ao_hbm, ax_hbm, wo_hbm, wx_hbm,
    mid_hbm, normed_hbm, act_hbm, slope_hbm, out_hbm, att_hbm, inv_hbm,
    x_v, num_v, den_v, q_v, att_v, inv_v, a_v, w_v, mid_v, normed_v, act_v, slope_v,
    x_sem, num_sem, q_sem, a_sem, w_sem, row_sem, chunk_sem,
):
    tokens, width = x_v.shape
    rows = min(256, tokens)
    n = tokens // rows
    half = width // 2
    pairs = width // PAIR
    here = [pl.ds(i * rows, rows) for i in range(n)]
    seqs = [pl.ds(b * seq, seq) for b in range(tokens // seq)]
    q_in = []
    for p in range(pairs):
        q_in.append(copy(mixed_hbm.at[:, pl.ds(p * QKV, PAIR)], q_v.at[:, pl.ds(p * PAIR, PAIR)], q_sem.at[p]))
    num_in = []
    for b, at in enumerate(seqs):
        num_in.append(
            [copy(num_hbm.at[at], num_v.at[at], num_sem.at[0, b]), copy(den_hbm.at[at], den_v.at[at], num_sem.at[1, b])]
        )
    into = [copy(hbm.at[:, pl.ds(3 * half, half)], a_v.at[i], a_sem.at[i]) for i, hbm in enumerate((ao_hbm, ax_hbm))]
    x_in = [copy(x_hbm.at[here[i]], x_v.at[here[i]], x_sem.at[i]) for i in range(n)]
    for c in range(4):
        hbm = wo_hbm if c < 2 else wx_hbm
        for kind in range(2):
            copy(hbm.at[kind, c % 2], w_v.at[kind, c], w_sem.at[kind, c])
    for made in q_in:
        made.wait()
    out = []
    ones = head_ones()
    for b, at in enumerate(seqs):
        for made in num_in[b]:
            made.wait()
        for p in range(pairs):
            lanes = pl.ds(p * PAIR, PAIR)
            c, s, c_sum, s_sum = unpacked(received(near_ref[b, (p + pairs // 2) % pairs], far_ref[b, p], flag_ref, b))
            q = relu(q_v[at, lanes]).astype(F32)
            qc, qs = q * col_ref[at, 0:1], q * col_ref[at, 1:2]
            num = num_v[at, lanes] + dot(
                jnp.concatenate([qc, qs], axis=1).astype(BF), jnp.concatenate([c, s], axis=0).astype(BF)
            )
            den = den_v[at, lanes] + dot((qc * c_sum + qs * s_sum).astype(BF), ones)
            inv = 1.0 / (den + 1.0)
            att_v[at, lanes] = (num * inv).astype(BF)
            inv_v[at, lanes] = inv.astype(BF)
        out.append(copy(att_v.at[at], att_hbm.at[at], num_sem.at[2, b]))
        out.append(copy(inv_v.at[at], inv_hbm.at[at], num_sem.at[3, b]))
    for made in into:
        made.wait()
    for i in range(n):
        x_in[i].wait()
        mid = x_v[here[i], :] + dot_t(att_v[here[i], :half], a_v[0]) + dot_t(att_v[here[i], half:], a_v[1])
        mid_v[here[i], :] = mid
        x_v[here[i], :] = mid
        xhat, _ = moments(mid)
        normed_v[here[i], :] = (xhat * par_ref[row : row + 1, :] + par_ref[row + 2 : row + 3, :]).astype(BF)
        out.append(copy(mid_v.at[here[i]], mid_hbm.at[here[i]], row_sem.at[0, i]))
        out.append(copy(normed_v.at[here[i]], normed_hbm.at[here[i]], row_sem.at[1, i]))

    @pl.loop(0, 4)
    def _(c):
        for kind in range(2):
            pltpu.make_async_copy(wo_hbm.at[kind, 0], w_v.at[kind, c], w_sem.at[kind, c]).wait()
        for i in range(n):
            act, slope = gelu_and_slope(dot(normed_v[here[i], :], w_v[0, c]))
            act_v[c, here[i], :] = act
            slope_v[c, here[i], :] = slope
            x_v[here[i], :] += dot_t(act, w_v[1, c])
        copy(act_v.at[c], act_hbm.at[c], chunk_sem.at[0, c])
        copy(slope_v.at[c], slope_hbm.at[c], chunk_sem.at[1, c])

    out.append(copy(x_v, out_hbm, row_sem.at[2, 0]))
    for c in range(4):
        pltpu.make_async_copy(act_v.at[c], act_hbm.at[c], chunk_sem.at[0, c]).wait()
        pltpu.make_async_copy(slope_v.at[c], slope_hbm.at[c], chunk_sem.at[1, c]).wait()
    for made in out:
        made.wait()


def hidden(x, params, row, intra, mixed, states, flags, col, w_att, w_hid, seq):
    tokens, width = x.shape
    chunk = w_hid[0].shape[3]
    pairs = width // PAIR
    n = tokens // min(256, tokens)
    dma = pltpu.SemaphoreType.DMA
    whole = lambda i: (0, 0)
    rows_of = lambda dtype: pltpu.VMEM((tokens, width), dtype)
    return run(
        partial(hidden_kernel, row, seq),
        (1,),
        [(flags, None, pltpu.SMEM), (params, params.shape, whole), (col, col.shape, whole)]
        + [(s, s.shape, lambda i: (0, 0, 0, 0)) for s in states]
        + [(a, None, pl.ANY) for a in (x, *intra, mixed, *w_att, *w_hid)],
        [
            ((tokens, width), F32, None, pl.ANY),
            ((tokens, width), BF, None, pl.ANY),
            ((4, tokens, chunk), BF, None, pl.ANY),
            ((4, tokens, chunk), BF, None, pl.ANY),
            ((tokens, width), F32, None, pl.ANY),
            ((tokens, width), BF, None, pl.ANY),
            ((tokens, width), BF, None, pl.ANY),
        ],
        scratch=[
            rows_of(F32), rows_of(F32), rows_of(F32), rows_of(BF), rows_of(BF), rows_of(BF),
            pltpu.VMEM((2, width, width // 2), BF),
            pltpu.VMEM((2, 4, width, chunk), BF),
            rows_of(F32), rows_of(BF),
            pltpu.VMEM((4, tokens, chunk), BF),
            pltpu.VMEM((4, tokens, chunk), BF),
            dma((n,)), dma((4, tokens // seq)), dma((pairs,)), dma((2,)), dma((2, 4)), dma((3, n)), dma((2, 4)),
        ],
        name="hidden",
    )


def hidden_sums(w_hbm, act_hbm, slope_hbm, sum_hbm, low_v, acc_v, normed_v, pre_v, act_v, slope_v, w_v, sum_v, w_sem, act_sem, sum_sem):
    tokens, width = low_v.shape
    rows = min(256, tokens)

    @pl.loop(0, 2)
    def _(c):
        for kind in range(2):
            pltpu.make_async_copy(w_hbm.at[kind, 0], w_v.at[kind, c], w_sem.at[kind, c]).wait()
        pltpu.make_async_copy(act_hbm.at[0], act_v.at[c], act_sem.at[0, c]).wait()
        pltpu.make_async_copy(slope_hbm.at[0], slope_v.at[c], act_sem.at[1, c]).wait()
        for i in range(tokens // rows):
            here = pl.ds(i * rows, rows)
            pre = (dot(low_v[here, :], w_v[1, c]) * slope_v[c, here, :].astype(F32)).astype(BF)
            pre_v[here, :] = pre
            acc_v[here, :] += dot_t(pre, w_v[0, c])
        sum_v[c, 1] = t_dot(low_v[...], act_v[c]).astype(BF)
        sum_v[c, 0] = t_dot(normed_v[...], pre_v[...]).astype(BF)
        for kind in range(2):
            copy(sum_v.at[c, kind], sum_hbm.at[kind, c], sum_sem.at[c, kind])


def start_hidden(w_hbm, act_hbm, slope_hbm, first, act_v, slope_v, w_v, w_sem, act_sem):
    for c in range(2):
        copy(w_hbm.at[1, c], w_v.at[1, c], w_sem.at[1, c])
        copy(slope_hbm.at[first + c], slope_v.at[c], act_sem.at[1, c])
        copy(w_hbm.at[0, c], w_v.at[0, c], w_sem.at[0, c])
        copy(act_hbm.at[first + c], act_v.at[c], act_sem.at[0, c])


def wait_sums(sum_v, sum_hbm, sum_sem):
    for c in range(2):
        for kind in range(2):
            pltpu.make_async_copy(sum_v.at[c, kind], sum_hbm.at[kind, c], sum_sem.at[c, kind]).wait()


def hidden_back_other_kernel(
    g_hbm, normed_hbm, act_hbm, slope_hbm, w_hbm,
    acc_hbm, sum_hbm,
    g_v, normed_v, act_v, slope_v, w_v, low_v, acc_v, pre_v, sum_v,
    g_sem, w_sem, act_sem, sum_sem,
):
    tokens, width = g_v.shape
    rows = min(256, tokens)
    n = tokens // rows
    here = [pl.ds(i * rows, rows) for i in range(n)]
    g_in = [copy(g_hbm.at[here[i]], g_v.at[here[i]], g_sem.at[i]) for i in range(n)]
    normed_in = copy(normed_hbm, normed_v, g_sem.at[n])
    start_hidden(w_hbm, act_hbm, slope_hbm, 2, act_v, slope_v, w_v, w_sem, act_sem)
    for i in range(n):
        g_in[i].wait()
        low_v[here[i], :] = g_v[here[i], :].astype(BF)
        acc_v[here[i], :] = jnp.zeros((rows, width), F32)
    normed_in.wait()
    hidden_sums(w_hbm, act_hbm, slope_hbm, sum_hbm, low_v, acc_v, normed_v, pre_v, act_v, slope_v, w_v, sum_v, w_sem, act_sem, sum_sem)
    out = copy(acc_v, acc_hbm, g_sem.at[0])
    wait_sums(sum_v, sum_hbm, sum_sem)
    out.wait()


def hidden_back_kernel(
    row, seq, par_ref, col_ref, g_hbm, acc_hbm, mid_hbm, normed_hbm, act_hbm, slope_hbm, w_hbm,
    ao_hbm, ax_hbm, mixed_hbm, att_hbm, inv_hbm,
    out_hbm, gn_hbm, norm_ref, state_ref, sum_hbm,
    g_v, mid_v, normed_v, act_v, slope_v, w_v, a_v, q_v, att_v, inv_v,
    low_v, acc_v, pre_v, sum_v, gn_v,
    g_sem, w_sem, act_sem, in_sem, q_sem, sum_sem, out_sem,
):
    tokens, width = g_v.shape
    rows = min(256, tokens)
    n = tokens // rows
    half = width // 2
    pairs = width // PAIR
    here = [pl.ds(i * rows, rows) for i in range(n)]
    g_in = [copy(g_hbm.at[here[i]], g_v.at[here[i]], g_sem.at[0, i]) for i in range(n)]
    acc_in = [copy(acc_hbm.at[here[i]], acc_v.at[here[i]], g_sem.at[1, i]) for i in range(n)]
    normed_in = copy(normed_hbm, normed_v, in_sem.at[0])
    start_hidden(w_hbm, act_hbm, slope_hbm, 0, act_v, slope_v, w_v, w_sem, act_sem)
    late = [
        copy(mid_hbm, mid_v, in_sem.at[1]),
        copy(att_hbm, att_v, in_sem.at[2]),
        copy(inv_hbm, inv_v, in_sem.at[3]),
    ]
    late += [copy(hbm.at[:, pl.ds(3 * half, half)], a_v.at[i], in_sem.at[4 + i]) for i, hbm in enumerate((ao_hbm, ax_hbm))]
    for p in range(pairs):
        late.append(copy(mixed_hbm.at[:, pl.ds(p * QKV, PAIR)], q_v.at[:, pl.ds(p * PAIR, PAIR)], q_sem.at[p]))
    norm_ref[...] = jnp.zeros_like(norm_ref)
    for i in range(n):
        g_in[i].wait()
        low_v[here[i], :] = g_v[here[i], :].astype(BF)
    for made in (*acc_in, normed_in):
        made.wait()
    hidden_sums(w_hbm, act_hbm, slope_hbm, sum_hbm, low_v, acc_v, normed_v, pre_v, act_v, slope_v, w_v, sum_v, w_sem, act_sem, sum_sem)
    for made in late:
        made.wait()
    out = []
    for i in range(n):
        grad = g_v[here[i], :] + norm_gradient(
            acc_v[here[i], :], mid_v[here[i], :], par_ref[row : row + 1, :], norm_ref
        )
        g_v[here[i], :] = grad
        out.append(copy(g_v.at[here[i]], out_hbm.at[here[i]], out_sem.at[0, i]))
        low = grad.astype(BF)
        inv = inv_v[here[i], :].astype(F32)
        gn_v[here[i], :half] = (dot(low, a_v[0]) * inv[:, :half]).astype(BF)
        gn_v[here[i], half:] = (dot(low, a_v[1]) * inv[:, half:]).astype(BF)
        out.append(copy(gn_v.at[here[i]], gn_hbm.at[here[i]], out_sem.at[1, i]))
    for b in range(tokens // seq):
        at = pl.ds(b * seq, seq)
        for p in range(pairs):
            lanes = pl.ds(p * PAIR, PAIR)
            gn = gn_v[at, lanes]
            e = dot((gn.astype(F32) * att_v[at, lanes].astype(F32)).astype(BF), head_ones())
            q = relu(q_v[at, lanes]).astype(F32)
            qc = (q * col_ref[at, 0:1]).astype(BF)
            qs = (q * col_ref[at, 1:2]).astype(BF)
            state_ref[b, p] = packed(
                t_dot(qc, gn),
                t_dot(qs, gn),
                -jnp.sum(qc.astype(F32) * e, axis=0, keepdims=True),
                -jnp.sum(qs.astype(F32) * e, axis=0, keepdims=True),
            )
    wait_sums(sum_v, sum_hbm, sum_sem)
    for made in out:
        made.wait()


def hidden_scratch(tokens, width, chunk):
    return [
        pltpu.VMEM((2, tokens, chunk), BF),
        pltpu.VMEM((2, tokens, chunk), BF),
        pltpu.VMEM((2, 2, width, chunk), BF),
    ]


def hidden_back_other(grad, saved, w_other):
    mid, normed, act, slope, mixed, att, inv = saved
    tokens, width = grad.shape
    chunk = w_other.shape[3]
    n = tokens // min(256, tokens)
    dma = pltpu.SemaphoreType.DMA
    rows_of = lambda dtype: pltpu.VMEM((tokens, width), dtype)
    return run(
        hidden_back_other_kernel,
        (1,),
        [(a, None, pl.ANY) for a in (grad, normed, act, slope, w_other)],
        [((tokens, width), F32, None, pl.ANY), ((2, 2, width, chunk), BF, None, pl.ANY)],
        scratch=[rows_of(F32), rows_of(BF)]
        + hidden_scratch(tokens, width, chunk)
        + [
            rows_of(BF), rows_of(F32),
            pltpu.VMEM((tokens, chunk), BF),
            pltpu.VMEM((2, 2, width, chunk), BF),
            dma((n + 1,)), dma((2, 2)), dma((2, 2)), dma((2, 2)),
        ],
        name="hidden_back_other",
    )


def hidden_back(grad, acc, params, row, saved, w_att, w_own, col, seq):
    mid, normed, act, slope, mixed, att, inv = saved
    tokens, width = grad.shape
    chunk = w_own.shape[3]
    pairs = width // PAIR
    n = tokens // min(256, tokens)
    dma = pltpu.SemaphoreType.DMA
    whole = lambda i: (0, 0)
    rows_of = lambda dtype: pltpu.VMEM((tokens, width), dtype)
    states = (tokens // seq, pairs, STATE_ROWS, PAIR)
    return run(
        partial(hidden_back_kernel, row, seq),
        (1,),
        [(params, params.shape, whole), (col, col.shape, whole)]
        + [(a, None, pl.ANY) for a in (grad, acc, mid, normed, act, slope, w_own, *w_att, mixed, att, inv)],
        [
            ((tokens, width), F32, None, pl.ANY),
            ((tokens, width), BF, None, pl.ANY),
            ((8, width), F32, (8, width), whole),
            (states, BF, states, lambda i: (0, 0, 0, 0)),
            ((2, 2, width, chunk), BF, None, pl.ANY),
        ],
        scratch=[rows_of(F32), rows_of(F32), rows_of(BF)]
        + hidden_scratch(tokens, width, chunk)
        + [
            pltpu.VMEM((2, width, width // 2), BF),
            rows_of(BF), rows_of(BF), rows_of(BF),
            rows_of(BF), rows_of(F32),
            pltpu.VMEM((tokens, chunk), BF),
            pltpu.VMEM((2, 2, width, chunk), BF),
            rows_of(BF),
            dma((2, n)), dma((2, 2)), dma((2, 2)), dma((6,)), dma((pairs,)), dma((2, 2)), dma((2, n)),
        ],
        name="hidden_back",
    )


def norm_gradient(grad, stream, gain, norm_ref):
    xhat, rstd = moments(stream)
    gx = grad * xhat
    norm_ref[0:1, :] += jnp.sum(gx, axis=0, keepdims=True)
    norm_ref[1:2, :] += jnp.sum(grad, axis=0, keepdims=True)
    g = grad * gain
    return rstd * (
        g - jnp.mean(g, axis=-1, keepdims=True) - xhat * jnp.mean(gx * gain, axis=-1, keepdims=True)
    )


def attend_back_kernel(
    flag_ref, col_ref, row_ref, mixed_ref, gn_ref, att_ref, near_ref, far_ref, out_ref, mask_ref, turned_ref,
):
    b, p = pl.program_id(0), pl.program_id(1)
    rows = mixed_ref.shape[0]

    @pl.when(p == 0)
    def _():
        cosine, same, t, u = mask_of(col_ref, row_ref)
        mask_ref[...] = jnp.where(same & (t >= u), cosine, 0.0)
        turned_ref[...] = jnp.where(same & (t <= u), cosine, 0.0)

    q = relu(mixed_ref[:, :PAIR])
    k = relu(mixed_ref[:, PAIR : 2 * PAIR])
    v = mixed_ref[:, 2 * PAIR :]
    gn = gn_ref[...]
    shape = (rows, PAIR)
    lo = low_lanes(shape)
    lane = lax.broadcasted_iota(jnp.int32, shape, 1)
    zero = jnp.zeros_like(q)
    e = dot((gn.astype(F32) * att_ref[...].astype(F32)).astype(BF), head_ones())
    v_one = jnp.concatenate([v, jnp.where(lane < 2, 1.0, 0.0).astype(BF)], axis=1)
    step = min(256, rows)
    gq_of, gk_of, gv_of = [], [], []
    for head in range(2):
        own = lo if head == 0 else ~lo
        k_own = jnp.where(own, k, zero)
        e_own = e if head == 0 else pltpu.roll(e, HD, 1)
        e_high = e_own.astype(BF)
        e_low = (e_own - e_high.astype(F32)).astype(BF)
        tail = jnp.where(lane == 0, -e_high, jnp.where(lane == 1, -e_low, zero))
        g_tail = jnp.concatenate([jnp.where(own, gn, zero), tail], axis=1)
        gq, gk, gv = [], [], []
        for at in range(0, rows, step):
            end = at + step
            gs = (dot_t(g_tail[at:end], v_one[:end]) * mask_ref[at:end, :end]).astype(BF)
            gq.append(dot(gs, k[:end]))
            turned = turned_ref[at:end, at:]
            w_t = (dot_t(k_own[at:end], q[at:]) * turned).astype(BF)
            gv.append(dot(w_t, gn[at:]))
            gs_t = (dot_t(v_one[at:end], g_tail[at:]) * turned).astype(BF)
            gk.append(dot(gs_t, q[at:]))
        gq_of.append(jnp.concatenate(gq, axis=0))
        gk_of.append(jnp.concatenate(gk, axis=0))
        gv_of.append(jnp.concatenate(gv, axis=0))

    c, s, c_sum, s_sum = unpacked(received(near_ref[0, 0], far_ref[0, 0], flag_ref, b))
    both = dot_t(gn, jnp.concatenate([c, s], axis=0).astype(BF))
    gq = jnp.where(lo, gq_of[0], gq_of[1])
    gq += col_ref[:, 0:1] * (both[:, :PAIR] - e * c_sum) + col_ref[:, 1:2] * (both[:, PAIR:] - e * s_sum)
    out_ref[:, :PAIR] = jnp.where(q > 0, gq, 0.0).astype(BF)
    out_ref[:, PAIR : 2 * PAIR] = jnp.where(lo, gk_of[0], gk_of[1]).astype(BF)
    out_ref[:, 2 * PAIR :] = jnp.where(lo, gv_of[0], gv_of[1]).astype(BF)


def attend_back(mixed, gn, att, near, far, flags, col, row, rows):
    grid = pair_grid(mixed, rows)
    pairs = grid[1]
    half = pairs // 2
    state = (1, 1, STATE_ROWS, PAIR)
    return run(
        attend_back_kernel,
        grid,
        [
            (flags, None, pltpu.SMEM),
            (col, (rows, col.shape[1]), lambda b, p: (b, 0)),
            (row, (row.shape[0], rows), lambda b, p: (0, b)),
            (mixed, (rows, QKV), lambda b, p: (b, p)),
            (gn, (rows, PAIR), lambda b, p: (b, p)),
            (att, (rows, PAIR), lambda b, p: (b, p)),
            (near, state, lambda b, p: (b, lax.rem(p + half, pairs), 0, 0)),
            (far, state, lambda b, p: (b, p, 0, 0)),
        ],
        [(mixed.shape, BF, (rows, QKV), lambda b, p: (b, p))],
        scratch=[pltpu.VMEM((rows, rows), F32), pltpu.VMEM((rows, rows), F32)],
        name="attend_back",
    )[0]


def regroup_pairs(tiles):
    lo = low_lanes(tiles[0].shape)
    first, second = [], []
    for a, b in zip(tiles[::2], tiles[1::2]):
        first.append(jnp.where(lo, a, pltpu.roll(b, HD, 1)))
        second.append(jnp.where(lo, pltpu.roll(a, HD, 1), b))
    return first, second


def project_sums_kernel(
    seq, flag_ref, col_ref, near_ref, far_ref, gm_hbm, mixed_hbm, g_hbm, normed_hbm, att_hbm,
    gm_out_hbm, sum_own_hbm, sum_other_hbm,
    gm_v, mixed_v, g_v, normed_v, att_v, low_v, sum_v,
    gm_sem, mixed_sem, in_sem, sum_sem, out_sem,
):
    tokens, width = g_v.shape
    half = gm_v.shape[2]
    pairs = half // QKV
    order = (1, 0)
    parts = [pl.ds(side * half, half) for side in range(2)]
    came = [None, None]
    for side in order:
        came[side] = [
            copy(gm_hbm.at[:, parts[side]], gm_v.at[side], gm_sem.at[side]),
            copy(mixed_hbm.at[:, parts[side]], mixed_v.at[side], mixed_sem.at[side]),
        ]
        if side == order[0]:
            normed_in = copy(normed_hbm, normed_v, in_sem.at[0])
            g_in = copy(g_hbm, g_v, in_sem.at[1])
            att_in = copy(att_hbm, att_v, in_sem.at[2])
    out = []
    for side, hbm in ((1, sum_other_hbm), (0, sum_own_hbm)):
        for made in came[side]:
            made.wait()
        for b in range(tokens // seq):
            at = slice(b * seq, (b + 1) * seq)
            for j in range(pairs):
                p = side * pairs + j
                k_at = slice(j * QKV + PAIR, j * QKV + 2 * PAIR)
                v_at = slice(j * QKV + 2 * PAIR, (j + 1) * QKV)
                st = received(near_ref[b, (p + pairs) % (2 * pairs)], far_ref[b, p], flag_ref, b)
                c, s, c_sum, s_sum = unpacked(st)
                both = jnp.concatenate([c, s], axis=0).astype(BF)
                k, v = relu(mixed_v[side, at, k_at]), mixed_v[side, at, v_at]
                memcos, memsin = col_ref[at, 2:3], col_ref[at, 3:4]
                toward = dot_t(v, both)
                gk = gm_v[side, at, k_at].astype(F32)
                gk += memcos * (toward[:, :PAIR] + c_sum) + memsin * (toward[:, PAIR:] + s_sum)
                gm_v[side, at, k_at] = jnp.where(k > 0, gk, 0.0).astype(BF)
                kf = k.astype(F32)
                features = jnp.concatenate([kf * memcos, kf * memsin], axis=1).astype(BF)
                gm_v[side, at, v_at] = (gm_v[side, at, v_at].astype(F32) + dot(features, both)).astype(BF)
        out.append(copy(gm_v.at[side], gm_out_hbm.at[:, parts[side]], out_sem.at[side]))
        if side == order[0]:
            for made in (normed_in, g_in, att_in):
                made.wait()
            low_v[...] = g_v[...].astype(BF)
        qkv = t_dot(normed_v[...], gm_v[side])
        o = t_dot(low_v[...], att_v[:, side * width // 2 : (side + 1) * width // 2])
        tiles = [
            qkv[:, (j * 3 + part) * PAIR : (j * 3 + part + 1) * PAIR] for part in range(3) for j in range(pairs)
        ] + [o[:, j * PAIR : (j + 1) * PAIR] for j in range(pairs)]
        for i, columns in enumerate(regroup_pairs(tiles)):
            for j, column in enumerate(columns):
                sum_v[side, i, :, j * PAIR : (j + 1) * PAIR] = column.astype(BF)
        out.append(copy(sum_v.at[side], hbm, sum_sem.at[side]))
    for made in out:
        made.wait()


def project_sums(gmixed, mixed, states, flags, col, grad, normed, att, seq):
    tokens, width = grad.shape
    half = gmixed.shape[1] // 2
    dma = pltpu.SemaphoreType.DMA
    whole = lambda i: (0, 0)
    sums = ((2, width, width), BF, None, pl.ANY)
    return run(
        partial(project_sums_kernel, seq),
        (1,),
        [(flags, None, pltpu.SMEM), (col, col.shape, whole)]
        + [(s, s.shape, lambda i: (0, 0, 0, 0)) for s in states]
        + [(a, None, pl.ANY) for a in (gmixed, mixed, grad, normed, att)],
        [(gmixed.shape, BF, None, pl.ANY), sums, sums],
        scratch=[
            pltpu.VMEM((2, tokens, half), BF),
            pltpu.VMEM((2, tokens, half), BF),
            pltpu.VMEM((tokens, width), F32),
            pltpu.VMEM((tokens, width), BF),
            pltpu.VMEM((tokens, width), BF),
            pltpu.VMEM((tokens, width), BF),
            pltpu.VMEM((2, 2, width, width), BF),
            dma((2,)), dma((2,)), dma((3,)), dma((2,)), dma((2,)),
        ],
        name="project_sums",
    )


def project_back_kernel(row, gm_ref, own_ref, other_ref, x_ref, par_ref, g_ref, out_ref, norm_ref):
    @pl.when(pl.program_id(0) == 0)
    def _():
        norm_ref[...] = jnp.zeros_like(norm_ref)

    half = own_ref.shape[1]
    grad = dot_t(gm_ref[:, :half], own_ref[...]) + dot_t(gm_ref[:, half:], other_ref[...])
    out_ref[...] = g_ref[...] + norm_gradient(grad, x_ref[...], par_ref[row : row + 1, :], norm_ref)


def project_back(gmixed, own, other, x, params, row, grad):
    tokens, width = x.shape
    half = gmixed.shape[1] // 2
    rows = min(256, tokens)
    whole = lambda i: (0, 0)
    by_row = lambda i: (i, 0)
    return run(
        partial(project_back_kernel, row),
        (tokens // rows,),
        [
            (gmixed, (rows, 2 * half), by_row),
            (own, (width, half), whole),
            (other, (width, half), whole),
            (x, (rows, width), by_row),
            (params, params.shape, whole),
            (grad, (rows, width), by_row),
        ],
        [
            ((tokens, width), F32, (rows, width), by_row),
            ((8, width), F32, (8, width), whole),
        ],
        name="project_back",
    )


def shards(
    layer_input,
    doc_lengths,
    ln1_gain,
    ln1_bias,
    qkv_weight,
    out_weight,
    ln2_gain,
    ln2_bias,
    in_weight,
    down_weight,
    cotangent,
):
    batches, rows, width = layer_input.shape
    layers = qkv_weight.shape[0]
    n_dp = lax.axis_size("dp")
    d, h = lax.axis_index("dp"), lax.axis_index("head")
    block = width // n_dp
    groups = xor_groups(n_dp)
    order = block_order(groups)
    tokens = batches * rows

    first_row = h * rows
    col, row, flags, back_flags = [], [], [], []
    for b in range(batches):
        lengths = doc_lengths[b]
        position = first_row + jnp.arange(rows, dtype=jnp.int32)
        doc, begin, size = places(lengths, position)
        angle = math.pi / 2 * (position - begin).astype(F32) / size.astype(F32)
        cos, sin = jnp.cos(angle), jnp.sin(angle)
        edges = first_row + jnp.array([-rows - 1, -1, 0, rows - 1, rows, 2 * rows], jnp.int32)
        at, _, _ = places(lengths, edges)
        first = (doc == at[2]).astype(F32)
        final = (doc == at[3]).astype(F32)
        place = doc.astype(F32)
        zero = jnp.zeros_like(cos)
        col.append(jnp.stack([first * cos, first * sin, final * cos, final * sin, cos, sin, place, zero], axis=1))
        row.append(jnp.stack([cos, sin, place, zero, zero, zero, zero, zero]))
        last = lax.axis_size("head") - 1
        near = (h >= 1) & (at[1] == at[2])
        far = (h >= 2) & (at[0] == at[2])
        flags.append(jnp.stack([near & (h != 2), near & (h == 2), far]))
        near = (h <= last - 1) & (at[3] == at[4])
        far = (h <= last - 2) & (at[3] == at[5])
        back_flags.append(jnp.stack([near & (h != 1), near & (h == 1), far]))
    col, row = jnp.concatenate(col), jnp.concatenate(row, axis=1)
    flags, back_flags = jnp.stack(flags).astype(F32), jnp.stack(back_flags).astype(F32)

    target = jnp.arange(width)
    source = (jnp.array(order)[target // block] ^ d) * block + target % block
    permutation = (jnp.arange(width)[:, None] == source[None, :]).astype(BF)
    x = dot(layer_input.reshape(tokens, width), permutation)
    cot = dot(cotangent.reshape(tokens, width), permutation)

    weights = []
    for l in range(layers):
        qkvo = jnp.concatenate([qkv_weight[l], out_weight[l].T], axis=1)
        updown = jnp.concatenate([in_weight[l], down_weight[l].T], axis=1)
        weights.append((Transfers(heads_steps(qkvo, groups)), Transfers(hidden_steps(updown, groups))))
    heads0, hidden0 = weights[0]
    start(heads0)

    params = jnp.concatenate([ln1_gain, ln1_bias, ln2_gain, ln2_bias], axis=0)[None]
    for masks in groups:
        params = spread(params, "dp", masks, 0)
    params = params.transpose(1, 0, 2).reshape(4 * layers, width).astype(F32)

    outer = len(groups) - 1
    stream = x
    for _ in range(outer):
        stream = advance(stream, heads0)
    start(hidden0)
    stream = advance(stream, heads0)
    stream = advance(stream, heads0)
    for _ in range(outer - 1):
        stream = advance(stream, hidden0)
    stream = advance(stream, heads0, hidden0)

    saved = []
    for l in range(layers):
        heads, units = weights[l]
        w_att = heads.result
        normed1, mixed, state = project(stream, params, l, *w_att, col, rows)
        states = Transfers(shift_steps(state, forward_shift))
        if l == 0:
            mixed = advance(mixed, units)
        start(states)
        if l + 1 < layers:
            nheads, nunits = weights[l + 1]
            start(nheads)
        intra = attend(mixed, col, row, rows)
        intra = advance(intra, states)
        if l + 1 < layers:
            for _ in range(outer):
                intra = advance(intra, nheads)
            start(nunits)
        intra = advance(intra, units)
        if l + 1 < layers:
            intra = advance(intra, nheads)
            for _ in range(outer):
                intra = advance(intra, nunits)
        intra = advance(intra, units)
        w_hid = units.result
        mid, normed2, act, slope, out, att, inv = hidden(
            stream, params, 2 * layers + l, intra, mixed, states.result, flags, col, w_att, w_hid, rows
        )
        saved.append((stream, normed1, states.result, (mid, normed2, act, slope, mixed, att, inv), w_att, w_hid))
        stream = out
        if l + 1 < layers:
            stream = advance(stream, nheads, nunits)
            stream = advance(stream, nheads)

    layer_output = dot_t(stream.astype(BF), permutation).astype(BF).reshape(layer_input.shape)

    def moving(chains):
        return [chain for chain in chains if chain.result is None]

    grad = cot
    sums = []
    norm_grads = [None] * layers
    for l in reversed(range(layers)):
        stream, normed1, states, kept, w_att, w_hid = saved[l]
        mixed, att = kept[4], kept[5]
        previous = sums[-1] if sums else ()
        acc, other = hidden_back_other(grad, kept, w_hid[1])
        acc = advance(acc, *moving(previous))
        mine = []
        hid_g = Transfers(
            sum_steps(other, lambda came, mine=mine: add(mine[0], came), lambda total: (total[1], total[0]), groups)
        )
        start(hid_g)
        grad, gn, norm2_g, gstate, own = hidden_back(
            grad, acc, params, 2 * layers + l, kept, w_att, w_hid[0], col, rows
        )
        mine.append(own)
        gstates = Transfers(shift_steps(gstate, backward_shift))
        start(gstates)
        gn = advance(gn, hid_g, *moving(previous))
        gmixed = attend_back(mixed, gn, att, *states, flags, col, row, rows)
        gmixed = advance(gmixed, gstates, hid_g, *moving(previous))
        gmixed, own, other = project_sums(
            gmixed, mixed, gstates.result, back_flags, col, grad, normed1, att, rows
        )
        att_g = Transfers(sum_steps(other, partial(add, own), lambda total: jnp.split(total, 2, axis=2), groups))
        start(att_g)
        grad, norm1_g = project_back(gmixed, *w_att, stream, params, l, grad)
        grad = advance(grad, att_g, hid_g)
        sums.append((hid_g, att_g))
        norm_grads[l] = (norm1_g[0], norm1_g[1], norm2_g[0], norm2_g[1])

    high = lax.reduce_precision(grad, 8, 7)
    input_grad = dot_t(high.astype(BF), permutation) + dot_t((grad - high).astype(BF), permutation)
    input_grad = input_grad.reshape(layer_input.shape)

    small = jnp.stack([norm_grads[l][i] for i in range(4) for l in range(layers)])
    small = small + swap(small, "head", 1)
    small = small + swap(small, "head", 2)
    small = small.reshape(4 * layers, n_dp, block).transpose(1, 0, 2)
    for masks in groups[::-1]:
        count = small.shape[0] // (len(masks) + 1)
        total = small[:count]
        for j, m in enumerate(masks):
            total = total + swap(small[(j + 1) * count : (j + 2) * count], "dp", m)
        small = total
    part = block // lax.axis_size("head")
    small = lax.dynamic_slice_in_dim(small.reshape(4, layers, block), h * part, part, 2)

    input_grad = finish(input_grad, [chain for layer in sums for chain in layer])
    sums = sums[::-1]
    third = sums[0][1].result.shape[1] * 3 // 4
    qkv_grad = jnp.stack([s[1].result[:, :third] for s in sums])
    out_grad = jnp.stack([s[1].result[:, third:].T for s in sums])
    units = sums[0][0].result.shape[1] // 2
    down_grad = jnp.stack([s[0].result[:, :units].T for s in sums])
    in_grad = jnp.stack([s[0].result[:, units:] for s in sums])
    return (
        layer_output,
        input_grad,
        small[0],
        small[1],
        qkv_grad,
        out_grad,
        small[2],
        small[3],
        in_grad,
        down_grad,
    )


def solution(mesh):
    in_specs = (
        P("dp", "head", None),
        P("dp", None),
        P(None, "dp"),
        P(None, "dp"),
        P(None, "dp", "head"),
        P(None, "head", "dp"),
        P(None, "dp"),
        P(None, "dp"),
        P(None, "dp", "head"),
        P(None, "head", "dp"),
        P("dp", "head", None),
    )
    out_specs = (
        P("dp", "head", None),
        P("dp", "head", None),
        P(None, ("dp", "head")),
        P(None, ("dp", "head")),
        P(None, "dp", "head"),
        P(None, "head", "dp"),
        P(None, ("dp", "head")),
        P(None, ("dp", "head")),
        P(None, "dp", "head"),
        P(None, "head", "dp"),
    )
    return jax.shard_map(shards, mesh=mesh, in_specs=in_specs, out_specs=out_specs, check_vma=False)
```
